128 devices in a mesh: ang: 16 (over z_lo, x, core), kslab: 8 (over z_hi, y).
Axes of the slice: x: 4, y: 4, z: 4 (z_hi: 2, z_lo: 2; z = z_hi * 2 + z_lo), core: 2. Of those that a mesh axis runs over, the one named last changes fastest.
Arguments:
- amplitude: bfloat16 [256, 112, 8, 2048], P('ang', None, 'kslab'), may hold values from -6 to 6
- ps_form: bfloat16 [2048, 896], replicated, may hold values from -0.125 to 0.125
- kgrid: float32 [8], replicated, may hold values from 0.1 to 3
- l_atom: int32 [112], replicated, may hold values from 0 to 7
- l_ps: int32 [112], replicated, may hold values from 0 to 7
- sixj: float32 [8, 12, 8, 8], replicated, may hold values from -0.5 to 0.5
Outputs:
- kernel: float32 [112, 8, 8, 896], P('ang', 'kslab')
The draws below stay inside these ranges and needn't reach their ends.
All inputs are finite; a program needn't handle non-finite values.
Results may differ from the reference program's by a relative error of at most 0.0003.
Values sent between devices are 32-bit elements; how exact they have to be, the bound alone decides.
No kernel may reach another device: no remote copies, remote signals or barrier semaphores. Data moves between devices by JAX's collectives and lax.ppermute only.
A program may use at most 128 MiB of HBM per device.

```python
import math
import jax
import jax.numpy as jnp
from jax import lax

NG = 256
NL = 12
NK = 8
M = 2048
LCH = 8
PS_CH = 112
ATOM_CH = 112
NJ = 8
COLS = 896


def touch_ends(array, stream_key, least, high):
    spot = [jax.random.randint(jax.random.fold_in(stream_key, axis), (), 0, length) for axis, length in enumerate(array.shape)]
    main_axis = array.shape.index(max(array.shape))
    next_to = spot[:main_axis] + [(spot[main_axis] + 1) % array.shape[main_axis]] + spot[main_axis + 1:]
    return array.at[tuple(spot)].set(least).at[tuple(next_to)].set(high)


def level_of(stream_key, dims, pieces, least, high):
    level, own = 1.0, jax.random.fold_in(stream_key, 6)
    for position, parts in pieces:
        draws = jnp.exp(jax.random.uniform(jax.random.fold_in(own, position), (parts,), jnp.float32, least / len(pieces), high / len(pieces)))
        level = level * jnp.repeat(draws, dims[position] // parts).reshape([-1 if axis == position else 1 for axis in range(len(dims))])
    return level


def noise(stream_key, extent, scale, most, split=(), kind=jnp.bfloat16):
    level = level_of(stream_key, extent, split, -0.22, 0.18) if split else 1.0
    drawn = jax.random.normal(stream_key, extent, jnp.float32) * scale * level
    return jnp.minimum(jnp.maximum(drawn, -most), most).astype(kind)


def setup_inputs(seed: int = 0) -> dict:
    seeds = jax.random.split(jax.random.key(seed), 7)
    return {
        "amplitude": noise(seeds[0], (NG, ATOM_CH, NK, M), 1.0, 6.0, ((0, 16), (2, 8))),
        "ps_form": noise(seeds[1], (M, COLS), M ** -0.5, 0.125),
        "kgrid": jnp.clip(jnp.exp(jax.random.uniform(seeds[2], (NK,), jnp.float32, math.log(0.1), math.log(3.0))), 0.1, 3.0),
        "l_atom": touch_ends(jax.random.randint(seeds[3], (ATOM_CH,), 0, LCH), jax.random.fold_in(seeds[3], 1), 0, LCH - 1).astype(jnp.int32),
        "l_ps": touch_ends(jax.random.randint(seeds[4], (PS_CH,), 0, LCH), jax.random.fold_in(seeds[4], 1), 0, LCH - 1).astype(jnp.int32),
        "sixj": jnp.clip(jax.random.uniform(seeds[5], (NJ, NL, LCH, LCH), jnp.float32, -0.5, 0.5), -0.5, 0.5),
    }


def legendre_table(first_row, row_count, total_points, degrees):
    positions = (first_row + jnp.arange(row_count)).astype(jnp.float32)
    angles = jnp.pi * (positions + 0.5) / total_points
    grid_nodes = jnp.cos(angles)
    grid_weights = (jnp.pi / total_points) * jnp.sin(angles)
    series = [jnp.ones_like(grid_nodes), grid_nodes]
    for degree in range(1, degrees - 1):
        series.append(((2 * degree + 1) * grid_nodes * series[-1] - degree * series[-2]) / (degree + 1))
    return grid_nodes, grid_weights[None, :] * jnp.stack(series[:degrees])


def reference(amplitude, ps_form, kgrid, l_atom, l_ps, sixj):
    grid_nodes, projector = legendre_table(0, NG, NG, NL)
    kcolumn = jnp.tile(kgrid, PS_CH)
    krow = kgrid[None, :, None]
    kcol = kcolumn[None, None, :]
    qinverse = 1.0 / (1.0 + krow * krow + kcol * kcol - 2.0 * grid_nodes[:, None, None] * krow * kcol)
    levels = jnp.arange(LCH, dtype=jnp.int32)
    onehot_ps = (l_ps[:, None] == levels[None, :]).astype(jnp.float32)

    def channel_kernel(channel):
        slab_data = lax.dynamic_index_in_dim(amplitude, channel, 1, keepdims=False)
        intersection = jnp.dot(slab_data.reshape(-1, M), ps_form, preferred_element_type=jnp.float32)
        intersection = intersection.reshape(NG, NK, COLS)
        values = jnp.einsum("lg,gkc->lkc", projector, intersection * qinverse, precision=lax.Precision.HIGHEST)
        atom_level = lax.dynamic_index_in_dim(l_atom, channel, 0, keepdims=False)
        onehot_atom = (levels == atom_level).astype(jnp.float32)
        coupling = jnp.einsum("jlxy,x,by->jlb", sixj, onehot_atom, onehot_ps, precision=lax.Precision.HIGHEST)
        widened = jnp.repeat(coupling, NK, axis=2)
        return jnp.einsum("jlc,lkc->jkc", widened, values, precision=lax.Precision.HIGHEST)

    return lax.map(channel_kernel, jnp.arange(ATOM_CH, dtype=jnp.int32))
```

```python
import functools
import math

import jax
import jax.numpy as jnp
from jax import lax
from jax.experimental import pallas as pl
from jax.experimental.pallas import tpu as pltpu
from jax.sharding import Mesh, PartitionSpec as P

F32 = jnp.float32
BF16 = jnp.bfloat16
LANES = 128
SUB = 8


def one_hot_lanes(rows, lanes, row_of, lane_of, dtype):
    r = lax.broadcasted_iota(jnp.int32, (rows, lanes), 0)
    c = lax.broadcasted_iota(jnp.int32, (rows, lanes), 1)
    return (row_of(r) == lane_of(c)).astype(dtype)


def build_tables(dims, place, kgrid, lps_ref, six_ref, r1_ref, pq_ref, x3_ref, w_ref):
    grid_count, total_points, degrees, levels, kpoints, ps_channels, columns = dims
    shape = (grid_count, LANES)
    first = place[0] * grid_count
    position = (first + lax.broadcasted_iota(jnp.int32, shape, 0)).astype(F32)
    theta = math.pi * (position + 0.5) / total_points
    node = jnp.cos(theta)
    weight = (math.pi / total_points) * jnp.sin(theta)
    kidx = lax.broadcasted_iota(jnp.int32, shape, 1) % kpoints
    kcol = jnp.zeros(shape, F32)
    for q in range(kpoints):
        kcol = jnp.where(kidx == q, kgrid[q], kcol)
    krow = kgrid[place[1]]
    qinverse = 1.0 / (1.0 + krow * krow + kcol * kcol - 2.0 * node * krow * kcol)
    scale = weight * qinverse
    series = [jnp.ones(shape, F32), node]
    for degree in range(1, degrees - 1):
        series.append(((2 * degree + 1) * node * series[-1] - degree * series[-2]) / (degree + 1))
    for degree in range(degrees):
        pq_ref[pl.ds(degree * grid_count, grid_count), :] = series[degree] * scale
    half = levels * kpoints
    spread = one_hot_lanes(levels, LANES, lambda r: r, lambda c: (c % half) // kpoints, F32)
    r1_ref[...] = jnp.dot(six_ref[...], spread, precision=lax.Precision.HIGHEST, preferred_element_type=F32)
    low = lax.broadcasted_iota(jnp.int32, (2 * SUB, LANES), 1) < half
    stride = degrees * levels
    for level in range(levels):
        coef = [r1_ref[pl.ds(degree * levels + level, SUB, stride=stride), :] for degree in range(degrees)]
        for pair in range(grid_count // 2):
            both = []
            for g in (2 * pair, 2 * pair + 1):
                acc = None
                for degree in range(degrees):
                    row = jnp.broadcast_to(pq_ref[pl.ds(degree * grid_count + g, 1), :], (SUB, LANES))
                    term = coef[degree] * row
                    acc = term if acc is None else acc + term
                both.append(acc)
            value = jnp.concatenate(both, axis=0)
            hi = value.astype(BF16).astype(F32)
            rest = value - hi
            mid = rest.astype(BF16).astype(F32)
            tail = rest - mid
            rows = pl.ds((level * grid_count + 2 * pair) * SUB, 2 * SUB)
            x3_ref[rows, 0:LANES] = jnp.where(low, hi, mid).astype(BF16)
            x3_ref[rows, LANES:2 * LANES] = jnp.where(low, tail, 0.0).astype(BF16)
    rep = one_hot_lanes(ps_channels, columns, lambda r: r, lambda c: c // kpoints, F32)
    level_of = jnp.dot(lps_ref[...].astype(F32), rep, preferred_element_type=F32)
    code = level_of.astype(jnp.int32) * kpoints + lax.broadcasted_iota(jnp.int32, (1, columns), 1) % kpoints
    r = lax.broadcasted_iota(jnp.int32, (2 * LANES, columns), 0)
    pick = ((r % half == code) & (r < 3 * half)).astype(F32).astype(BF16)
    w_ref[...] = jnp.dot(x3_ref[...], pick, preferred_element_type=F32)


def kernel_body(dims, geometry, place, l_atom, kgrid, lps_ref, six_ref, a_ref, ps_ref, send_ref, keep_ref,
                i_ref, w_ref, r1_ref, pq_ref, x3_ref):
    grid_count, total_points, degrees, levels, kpoints, ps_channels, columns = dims
    channels, owned, groups, block = geometry
    step = pl.program_id(0)

    @pl.when(step == 0)
    def _():
        build_tables(dims, place, kgrid, lps_ref, six_ref, r1_ref, pq_ref, x3_ref, w_ref)

    rows = block * channels
    product = jnp.dot(a_ref[...].reshape(rows, a_ref.shape[-1]), ps_ref[...], preferred_element_type=F32)
    for t in range(columns // LANES):
        i_ref[t, pl.ds(pl.multiple_of(step * rows, rows), rows), :] = product[:, t * LANES:(t + 1) * LANES]

    @pl.when(step == pl.num_programs(0) - 1)
    def _():
        tiles = columns // LANES
        chunk = tiles * SUB
        for slot, out_ref in ((0, send_ref), (1, keep_ref)):
            core = place[2] if slot == 1 else 1 - place[2]

            def group(d, carry):
                for r in range(owned):
                    a = d * (2 * owned) + core * owned + r
                    base = l_atom[a] * (grid_count * SUB)
                    acc = [None] * tiles
                    for g in range(grid_count):
                        for t in range(tiles):
                            cols = slice(t * LANES, (t + 1) * LANES)
                            coef = w_ref[pl.ds(pl.multiple_of(base + g * SUB, SUB), SUB), cols]
                            row = i_ref[t, pl.ds(g * channels + a, SUB, stride=0), :]
                            term = coef * row
                            acc[t] = term if acc[t] is None else acc[t] + term
                    for t in range(tiles):
                        out_ref[pl.ds(d * (SUB * chunk) + t * SUB + r, SUB, stride=chunk), :] = acc[t]
                return carry

            lax.fori_loop(0, groups, group, 0)


def partial_kernel(amplitude, ps_form, kgrid, l_atom, l_ps, sixj, place, total_points):
    grid_count, channels, radial = amplitude.shape
    columns = ps_form.shape[1]
    kpoints = kgrid.shape[0]
    total_j, degrees, levels, _ = sixj.shape
    ps_channels = l_ps.shape[0]
    owned = channels * grid_count // total_points
    groups = channels // (2 * owned)
    block = 4
    dims = (grid_count, total_points, degrees, levels, kpoints, ps_channels, columns)
    geometry = (channels, owned, groups, block)
    out = jax.ShapeDtypeStruct((groups * total_j * SUB * columns // LANES, LANES), F32)
    smem = pl.BlockSpec(memory_space=pltpu.SMEM)

    def whole(shape):
        return pl.BlockSpec(shape, lambda i: (0,) * len(shape), pipeline_mode=pl.Buffered(1))

    six = sixj.reshape(-1, levels)
    return pl.pallas_call(
        functools.partial(kernel_body, dims, geometry),
        grid=(grid_count // block,),
        in_specs=[
            smem, smem, smem,
            whole((1, ps_channels)),
            whole(six.shape),
            pl.BlockSpec((block, channels, radial), lambda i: (i, 0, 0)),
            whole(ps_form.shape),
        ],
        out_specs=[pl.BlockSpec(out.shape, lambda i: (0, 0))] * 2,
        out_shape=[out, out],
        scratch_shapes=[
            pltpu.VMEM((columns // LANES, grid_count * channels, LANES), F32),
            pltpu.VMEM((levels * grid_count * SUB, columns), F32),
            pltpu.VMEM((six.shape[0], LANES), F32),
            pltpu.VMEM((degrees * grid_count, LANES), F32),
            pltpu.VMEM((levels * grid_count * SUB, 2 * LANES), BF16),
        ],
        compiler_params=pltpu.CompilerParams(
            dimension_semantics=("arbitrary",), vmem_limit_bytes=56 * 1024 * 1024
        ),
        name="recoupled_partials",
    )(place, l_atom, kgrid, l_ps.reshape(1, -1), six, amplitude, ps_form)


def local(amplitude, ps_form, kgrid, l_atom, l_ps, sixj):
    grid_count, channels, slab_points, radial = amplitude.shape
    columns = ps_form.shape[1]
    total_j = sixj.shape[0]
    ang_size = lax.axis_size(("zl", "x", "core"))
    owned = channels // ang_size
    groups = ang_size // 2
    place = jnp.stack(
        [lax.axis_index(("zl", "x", "core")), lax.axis_index(("zh", "y")), lax.axis_index("core")]
    ).astype(jnp.int32)
    send, keep = partial_kernel(
        amplitude.reshape(grid_count, channels, radial), ps_form, kgrid, l_atom, l_ps, sixj, place,
        grid_count * ang_size,
    )
    mine = keep + lax.ppermute(send, "core", [(0, 1), (1, 0)])
    tiles = columns // LANES
    mine = mine.reshape(groups * total_j, tiles * SUB, LANES)
    got = lax.all_to_all(mine, ("zl", "x", "zh", "y"), split_axis=0, concat_axis=0, tiled=True)
    total = jnp.sum(got.reshape(groups, total_j, tiles, SUB, LANES), axis=0)
    return jnp.transpose(total[:, :, :owned], (2, 0, 1, 3)).reshape(owned, 1, total_j, columns)


def solution(mesh):
    fine = Mesh(mesh.devices.reshape(2, 4, 2, 2, 4), ("zl", "x", "core", "zh", "y"))
    ang, slab = ("zl", "x", "core"), ("zh", "y")
    in_specs = (P(ang, None, slab, None), P(), P(), P(), P(), P())
    out_specs = P(ang, slab, None, None)
    return jax.shard_map(local, mesh=fine, in_specs=in_specs, out_specs=out_specs, check_vma=False)
```

```python
import functools
import math

import jax
import jax.numpy as jnp
from jax import lax
from jax.experimental import pallas as pl
from jax.experimental.pallas import tpu as pltpu
from jax.sharding import Mesh, PartitionSpec as P

F32 = jnp.float32
BF16 = jnp.bfloat16
LANES = 128
SUB = 8
CHUNK = 2
BLOCK = 4
VMEM_LIMIT = 56 * 1024 * 1024


def iota(shape, axis):
    return lax.broadcasted_iota(jnp.int32, shape, axis)


def build_tables(dims, place, kgrid, lps_ref, six_ref, r1_ref, pq_ref, x3_ref, w_ref):
    grid_count, total_points, degrees, levels, kpoints, ps_channels, columns = dims
    shape = (grid_count, LANES)
    position = (place[0] * grid_count + iota(shape, 0)).astype(F32)
    theta = math.pi * (position + 0.5) / total_points
    node = jnp.cos(theta)
    weight = (math.pi / total_points) * jnp.sin(theta)
    kidx = iota(shape, 1) % kpoints
    kcol = jnp.zeros(shape, F32)
    for q in range(kpoints):
        kcol = jnp.where(kidx == q, kgrid[q], kcol)
    krow = kgrid[place[1]]
    qinverse = 1.0 / (1.0 + krow * krow + kcol * kcol - 2.0 * node * krow * kcol)
    scale = weight * qinverse
    series = [jnp.ones(shape, F32), node]
    for degree in range(1, degrees - 1):
        series.append(((2 * degree + 1) * node * series[-1] - degree * series[-2]) / (degree + 1))
    for degree in range(degrees):
        pq_ref[pl.ds(degree * grid_count, grid_count), :] = series[degree] * scale
    half = levels * kpoints
    pad = 2 * SUB
    eye = (iota((pad, degrees), 0) == iota((pad, degrees), 1)).astype(F32)
    turned = lax.dot_general(
        eye, six_ref[...], (((1,), (1,)), ((), ())), precision=lax.Precision.HIGHEST, preferred_element_type=F32
    )
    pairs = levels * levels
    turned = jnp.concatenate([turned[:, j * pairs:(j + 1) * pairs] for j in range(SUB)], axis=0)
    spread_shape = (pairs, levels * LANES)
    source = iota(spread_shape, 0)
    target = iota(spread_shape, 1)
    wanted = (target // LANES) * levels + (target % half) // kpoints
    spread = (source == wanted).astype(F32)
    expanded = jnp.dot(turned, spread, precision=lax.Precision.HIGHEST, preferred_element_type=F32)
    for level in range(levels):
        r1_ref[level] = expanded[:, level * LANES:(level + 1) * LANES]
    low = iota((2 * SUB, LANES), 1) < half
    for level in range(levels):
        coef = [r1_ref[level, pl.ds(degree, SUB, stride=pad), :] for degree in range(degrees)]
        for pair in range(grid_count // 2):
            both = []
            for g in (2 * pair, 2 * pair + 1):
                acc = None
                for degree in range(degrees):
                    row = pq_ref[pl.ds(degree * grid_count + g, SUB, stride=0), :]
                    term = coef[degree] * row
                    acc = term if acc is None else acc + term
                both.append(acc)
            value = jnp.concatenate(both, axis=0)
            hi = value.astype(BF16).astype(F32)
            rest = value - hi
            mid = rest.astype(BF16).astype(F32)
            tail = rest - mid
            rows = pl.ds((level * grid_count + 2 * pair) * SUB, 2 * SUB)
            x3_ref[rows, 0:LANES] = jnp.where(low, hi, mid).astype(BF16)
            x3_ref[rows, LANES:2 * LANES] = jnp.where(low, tail, 0.0).astype(BF16)
    rep_shape = (ps_channels, columns)
    rep = (iota(rep_shape, 0) == iota(rep_shape, 1) // kpoints).astype(F32)
    level_of = jnp.dot(lps_ref[...].astype(F32), rep, preferred_element_type=F32)
    code = level_of.astype(jnp.int32) * kpoints + iota((1, columns), 1) % kpoints
    r = iota((2 * LANES, columns), 0)
    pick = ((r % half == code) & (r < 3 * half)).astype(F32).astype(BF16)
    w_ref[...] = jnp.dot(x3_ref[...], pick, preferred_element_type=F32)


def recouple_group(geometry, l_atom, i_ref, w_ref, out_ref, first_tile, count, core, d):
    grid_count, channels, owned, groups, tiles = geometry
    rows = tiles * owned
    for r in range(owned):
        a = (2 * d + core) * owned + r
        base = l_atom[a] * (grid_count * SUB)
        acc = [None] * count
        for g in range(grid_count):
            for t in range(count):
                lo = (first_tile + t) * LANES
                coef = w_ref[pl.ds(pl.multiple_of(base + g * SUB, SUB), SUB), lo:lo + LANES]
                term = coef * i_ref[t, pl.ds(g * channels + a, SUB, stride=0), :]
                acc[t] = term if acc[t] is None else acc[t] + term
        for t in range(count):
            out_ref[pl.ds(d * (SUB * rows) + (first_tile + t) * owned + r, SUB, stride=rows), :] = acc[t]


def tile_chunks(tiles):
    return [(t, min(CHUNK, tiles - t)) for t in range(0, tiles, CHUNK)]


def first_body(dims, geometry, l_atom, kgrid, lps_ref, six_ref, a_hbm, ps_hbm, *rest):
    grid_count, channels, owned, groups, tiles = geometry
    chunks = tile_chunks(tiles)
    send_ref, w_ref = rest[:2]
    i_refs = rest[2:2 + len(chunks)]
    a_ref, ps_ref, r1_ref, pq_ref, x3_ref, a_sems, ps_sem = rest[2 + len(chunks):]
    core = lax.axis_index("core")
    ang = (lax.axis_index("zl") * lax.axis_size("x") + lax.axis_index("x")) * lax.axis_size("core") + core
    slab = lax.axis_index("zh") * lax.axis_size("y") + lax.axis_index("y")

    def copy_a(m):
        block = pl.ds(m * BLOCK, BLOCK)
        return pltpu.make_async_copy(a_hbm.at[block], a_ref.at[block], a_sems.at[m])

    copy_ps = pltpu.make_async_copy(ps_hbm, ps_ref, ps_sem)
    copy_ps.start()
    steps = grid_count // BLOCK
    for m in range(steps):
        copy_a(m).start()
    build_tables(dims, (ang, slab), kgrid, lps_ref, six_ref, r1_ref, pq_ref, x3_ref, w_ref)
    copy_ps.wait()
    rows = BLOCK * channels
    radial = a_ref.shape[-1]
    per_step = groups // steps
    for n, (first_tile, count) in enumerate(chunks):
        def step(m, carry, n=n, first_tile=first_tile, count=count):
            if n == 0:
                copy_a(m).wait()
            left = a_ref[pl.ds(m * BLOCK, BLOCK)].reshape(rows, radial)
            product = jnp.dot(
                left, ps_ref[:, first_tile * LANES:(first_tile + count) * LANES], preferred_element_type=F32
            )
            if n > 0:
                for s in range(per_step):
                    recouple_group(
                        geometry, l_atom, i_refs[n - 1], w_ref, send_ref, *chunks[n - 1], 1 - core, m * per_step + s
                    )
            for t in range(count):
                i_refs[n][t, pl.ds(pl.multiple_of(m * rows, rows), rows), :] = product[:, t * LANES:(t + 1) * LANES]
            return carry

        lax.fori_loop(0, steps, step, 0)

    def last(d, carry):
        recouple_group(geometry, l_atom, i_refs[-1], w_ref, send_ref, *chunks[-1], 1 - core, d)
        return carry

    lax.fori_loop(0, groups, last, 0)


def second_body(geometry, l_atom, w_ref, *rest):
    groups, tiles = geometry[3:]
    chunks = tile_chunks(tiles)
    keep_ref = rest[-1]
    core = lax.axis_index("core")

    def group(d, carry):
        for n, chunk in enumerate(chunks):
            recouple_group(geometry, l_atom, rest[n], w_ref, keep_ref, *chunk, core, d)
        return carry

    lax.fori_loop(0, groups, group, 0)


def sum_body(owned, tiles, sources, total_j, got_ref, out_ref):
    rows = owned * tiles
    for r in range(owned):
        for t in range(tiles):
            acc = None
            for s in range(sources):
                part = got_ref[pl.ds(s * total_j * rows + t * owned + r, total_j, stride=rows), :]
                acc = part if acc is None else acc + part
            out_ref[r, :, t * LANES:(t + 1) * LANES] = acc


def local(amplitude, ps_form, kgrid, l_atom, l_ps, sixj):
    grid_count, channels, slab_points, radial = amplitude.shape
    columns = ps_form.shape[1]
    kpoints = kgrid.shape[0]
    total_j, degrees, levels, _ = sixj.shape
    ps_channels = l_ps.shape[0]
    ang_size = lax.axis_size(("zl", "x", "core"))
    owned = channels // ang_size
    groups = ang_size // 2
    tiles = columns // LANES
    dims = (grid_count, grid_count * ang_size, degrees, levels, kpoints, ps_channels, columns)
    geometry = (grid_count, channels, owned, groups, tiles)
    smem = pl.BlockSpec(memory_space=pltpu.SMEM)
    vmem = pl.BlockSpec(memory_space=pltpu.VMEM)
    hbm = pl.BlockSpec(memory_space=pl.ANY)
    params = pltpu.CompilerParams(vmem_limit_bytes=VMEM_LIMIT)
    part = jax.ShapeDtypeStruct((groups * total_j * tiles * owned, LANES), F32)
    chunks = tile_chunks(tiles)
    table_rows = levels * grid_count * SUB
    six = jnp.transpose(sixj, (0, 2, 3, 1)).reshape(-1, degrees)
    products = [jax.ShapeDtypeStruct((count, grid_count * channels, LANES), F32) for _, count in chunks]
    first = pl.pallas_call(
        functools.partial(first_body, dims, geometry),
        in_specs=[smem, smem, vmem, vmem, hbm, hbm],
        out_specs=[vmem] * (2 + len(chunks)),
        out_shape=[part, jax.ShapeDtypeStruct((table_rows, columns), F32), *products],
        scratch_shapes=[
            pltpu.VMEM((grid_count, channels, radial), BF16),
            pltpu.VMEM(ps_form.shape, BF16),
            pltpu.VMEM((levels, 2 * SUB * total_j, LANES), F32),
            pltpu.VMEM((degrees * grid_count, LANES), F32),
            pltpu.VMEM((table_rows, 2 * LANES), BF16),
            pltpu.SemaphoreType.DMA((grid_count // BLOCK,)),
            pltpu.SemaphoreType.DMA(()),
        ],
        compiler_params=params,
        name="first_half",
    )
    send, table, *products = first(
        l_atom, kgrid, l_ps.reshape(1, -1), six, amplitude.reshape(grid_count, channels, radial), ps_form
    )
    other = lax.ppermute(send, "core", [(0, 1), (1, 0)])
    keep = pl.pallas_call(
        functools.partial(second_body, geometry),
        in_specs=[smem] + [vmem] * (1 + len(chunks)),
        out_specs=vmem,
        out_shape=part,
        compiler_params=params,
        name="second_half",
    )(l_atom, table, *products)
    mine = (keep + other).reshape(groups * total_j, tiles * owned, 1, LANES)
    got = lax.all_to_all(mine, ("zl", "x", "zh", "y"), split_axis=0, concat_axis=0, tiled=True)
    total = pl.pallas_call(
        functools.partial(sum_body, owned, tiles, groups, total_j),
        in_specs=[vmem],
        out_specs=vmem,
        out_shape=jax.ShapeDtypeStruct((owned, total_j, columns), F32),
        compiler_params=params,
        name="sum_sources",
    )(got.reshape(part.shape))
    return total[:, None]


def solution(mesh):
    fine = Mesh(mesh.devices.reshape(2, 4, 2, 2, 4), ("zl", "x", "core", "zh", "y"))
    ang, slab = ("zl", "x", "core"), ("zh", "y")
    in_specs = (P(ang, None, slab, None), P(), P(), P(), P(), P())
    out_specs = P(ang, slab, None, None)
    return jax.shard_map(local, mesh=fine, in_specs=in_specs, out_specs=out_specs, check_vma=False)
```

```python
import functools
import math

import jax
import jax.numpy as jnp
from jax import lax
from jax.experimental import pallas as pl
from jax.experimental.pallas import tpu as pltpu
from jax.sharding import Mesh, PartitionSpec as P

F32 = jnp.float32
BF16 = jnp.bfloat16
LANES = 128
SUB = 8
CHUNK = 7
BLOCK = 8
VMEM_LIMIT = 28 * 1024 * 1024


def iota(shape, axis):
    return lax.broadcasted_iota(jnp.int32, shape, axis)


def build_tables(dims, place, kgrid, lps_ref, six_ref, r1_ref, pq_ref, x3_ref, w_ref):
    grid_count, total_points, degrees, levels, kpoints, ps_channels, columns = dims
    shape = (grid_count, LANES)
    position = (place[0] * grid_count + iota(shape, 0)).astype(F32)
    theta = math.pi * (position + 0.5) / total_points
    node = jnp.cos(theta)
    weight = (math.pi / total_points) * jnp.sin(theta)
    kidx = iota(shape, 1) % kpoints
    kcol = jnp.zeros(shape, F32)
    for q in range(kpoints):
        kcol = jnp.where(kidx == q, kgrid[q], kcol)
    krow = kgrid[place[1]]
    qinverse = 1.0 / (1.0 + krow * krow + kcol * kcol - 2.0 * node * krow * kcol)
    scale = weight * qinverse
    series = [jnp.ones(shape, F32), node]
    for degree in range(1, degrees - 1):
        series.append(((2 * degree + 1) * node * series[-1] - degree * series[-2]) / (degree + 1))
    for degree in range(degrees):
        pq_ref[pl.ds(degree * grid_count, grid_count), :] = series[degree] * scale
    half = levels * kpoints
    pad = 2 * SUB
    eye = (iota((pad, degrees), 0) == iota((pad, degrees), 1)).astype(F32)
    turned = lax.dot_general(
        eye, six_ref[...], (((1,), (1,)), ((), ())), precision=lax.Precision.HIGHEST, preferred_element_type=F32
    )
    pairs = levels * levels
    turned = jnp.concatenate([turned[:, j * pairs:(j + 1) * pairs] for j in range(SUB)], axis=0)
    spread_shape = (pairs, levels * LANES)
    source = iota(spread_shape, 0)
    target = iota(spread_shape, 1)
    wanted = (target // LANES) * levels + (target % half) // kpoints
    spread = (source == wanted).astype(F32)
    expanded = jnp.dot(turned, spread, precision=lax.Precision.HIGHEST, preferred_element_type=F32)
    for level in range(levels):
        r1_ref[level] = expanded[:, level * LANES:(level + 1) * LANES]
    low = iota((2 * SUB, LANES), 1) < half
    for level in range(levels):
        coef = [r1_ref[level, pl.ds(degree, SUB, stride=pad), :] for degree in range(degrees)]
        for pair in range(grid_count // 2):
            both = []
            for g in (2 * pair, 2 * pair + 1):
                acc = None
                for degree in range(degrees):
                    row = pq_ref[pl.ds(degree * grid_count + g, SUB, stride=0), :]
                    term = coef[degree] * row
                    acc = term if acc is None else acc + term
                both.append(acc)
            value = jnp.concatenate(both, axis=0)
            hi = value.astype(BF16).astype(F32)
            rest = value - hi
            mid = rest.astype(BF16).astype(F32)
            tail = rest - mid
            rows = pl.ds((level * grid_count + 2 * pair) * SUB, 2 * SUB)
            x3_ref[rows, 0:LANES] = jnp.where(low, hi, mid).astype(BF16)
            x3_ref[rows, LANES:2 * LANES] = jnp.where(low, tail, 0.0).astype(BF16)
    rep_shape = (ps_channels, columns)
    rep = (iota(rep_shape, 0) == iota(rep_shape, 1) // kpoints).astype(F32)
    level_of = jnp.dot(lps_ref[...].astype(F32), rep, preferred_element_type=F32)
    code = level_of.astype(jnp.int32) * kpoints + iota((1, columns), 1) % kpoints
    r = iota((2 * LANES, columns), 0)
    pick = ((r % half == code) & (r < 3 * half)).astype(F32).astype(BF16)
    w_ref[...] = jnp.dot(x3_ref[...], pick, preferred_element_type=F32)


def recouple_group(geometry, l_atom, i_ref, w_ref, out_ref, first_tile, count, core, d):
    grid_count, channels, owned, groups, tiles = geometry
    rows = tiles * owned
    for r in range(owned):
        a = (2 * d + core) * owned + r
        base = l_atom[a] * (grid_count * SUB)
        acc = [None] * count
        for g in range(grid_count):
            for t in range(count):
                lo = (first_tile + t) * LANES
                coef = w_ref[pl.ds(pl.multiple_of(base + g * SUB, SUB), SUB), lo:lo + LANES]
                term = coef * i_ref[t, pl.ds(g * channels + a, SUB, stride=0), :]
                acc[t] = term if acc[t] is None else acc[t] + term
        for t in range(count):
            out_ref[pl.ds(d * (SUB * rows) + (first_tile + t) * owned + r, SUB, stride=rows), :] = acc[t]


def tile_chunks(tiles):
    return [(t, min(CHUNK, tiles - t)) for t in range(0, tiles, CHUNK)]


def first_body(dims, geometry, la_hbm, kg_hbm, lps_hbm, six_hbm, a_hbm, ps_hbm, *rest):
    grid_count, channels, owned, groups, tiles = geometry
    chunks = tile_chunks(tiles)
    send_ref, w_ref = rest[:2]
    i_refs = rest[2:2 + len(chunks)]
    l_atom, kgrid, lps_ref, six_ref, a_ref, ps_ref, r1_ref, pq_ref, x3_ref, sems, a_sems = rest[2 + len(chunks):]
    core = lax.axis_index("core")
    ang = (lax.axis_index("zl") * lax.axis_size("x") + lax.axis_index("x")) * lax.axis_size("core") + core
    slab = lax.axis_index("zh") * lax.axis_size("y") + lax.axis_index("y")

    def copy_a(m):
        block = pl.ds(m * BLOCK, BLOCK)
        return pltpu.make_async_copy(a_hbm.at[block], a_ref.at[block], a_sems.at[m])

    pairs = ((kg_hbm, kgrid), (six_hbm, six_ref), (lps_hbm, lps_ref), (la_hbm, l_atom), (ps_hbm, ps_ref))
    small = [pltpu.make_async_copy(source, target, sems.at[i]) for i, (source, target) in enumerate(pairs)]
    for copy in small:
        copy.start()
    steps = grid_count // BLOCK
    for m in range(steps):
        copy_a(m).start()
    for copy in small[:3]:
        copy.wait()
    build_tables(dims, (ang, slab), kgrid, lps_ref, six_ref, r1_ref, pq_ref, x3_ref, w_ref)
    for copy in small[3:]:
        copy.wait()
    rows = BLOCK * channels
    radial = a_ref.shape[-1]
    per_step = groups // steps
    for n, (first_tile, count) in enumerate(chunks):
        def step(m, carry, n=n, first_tile=first_tile, count=count):
            if n == 0:
                copy_a(m).wait()
            left = a_ref[pl.ds(m * BLOCK, BLOCK)].reshape(rows, radial)
            product = jnp.dot(
                left, ps_ref[:, first_tile * LANES:(first_tile + count) * LANES], preferred_element_type=F32
            )
            if n > 0:
                for s in range(per_step):
                    recouple_group(
                        geometry, l_atom, i_refs[n - 1], w_ref, send_ref, *chunks[n - 1], 1 - core, m * per_step + s
                    )
            for t in range(count):
                i_refs[n][t, pl.ds(pl.multiple_of(m * rows, rows), rows), :] = product[:, t * LANES:(t + 1) * LANES]
            return carry

        lax.fori_loop(0, steps, step, 0)

    def last(d, carry):
        recouple_group(geometry, l_atom, i_refs[-1], w_ref, send_ref, *chunks[-1], 1 - core, d)
        return carry

    lax.fori_loop(0, groups, last, 0)


def second_body(geometry, l_atom, w_ref, *rest):
    groups, tiles = geometry[3:]
    chunks = tile_chunks(tiles)
    keep_ref = rest[-1]
    core = lax.axis_index("core")

    def group(d, carry):
        for n, chunk in enumerate(chunks):
            recouple_group(geometry, l_atom, rest[n], w_ref, keep_ref, *chunk, core, d)
        return carry

    lax.fori_loop(0, groups, group, 0)


def sum_body(owned, tiles, sources, total_j, got_ref, out_ref):
    rows = owned * tiles
    for r in range(owned):
        for t in range(tiles):
            acc = None
            for s in range(sources):
                part = got_ref[pl.ds(s * total_j * rows + t * owned + r, total_j, stride=rows), :]
                acc = part if acc is None else acc + part
            out_ref[r, :, t * LANES:(t + 1) * LANES] = acc


def local(amplitude, ps_form, kgrid, l_atom, l_ps, sixj):
    grid_count, channels, slab_points, radial = amplitude.shape
    columns = ps_form.shape[1]
    kpoints = kgrid.shape[0]
    total_j, degrees, levels, _ = sixj.shape
    ps_channels = l_ps.shape[0]
    ang_size = lax.axis_size(("zl", "x", "core"))
    owned = channels // ang_size
    groups = ang_size // 2
    tiles = columns // LANES
    dims = (grid_count, grid_count * ang_size, degrees, levels, kpoints, ps_channels, columns)
    geometry = (grid_count, channels, owned, groups, tiles)
    smem = pl.BlockSpec(memory_space=pltpu.SMEM)
    vmem = pl.BlockSpec(memory_space=pltpu.VMEM)
    hbm = pl.BlockSpec(memory_space=pltpu.HBM)
    params = pltpu.CompilerParams(vmem_limit_bytes=VMEM_LIMIT)
    part = pltpu.VMEM((groups * total_j * tiles * owned, LANES), F32)
    chunks = tile_chunks(tiles)
    table_rows = levels * grid_count * SUB
    six = jnp.transpose(sixj, (0, 2, 3, 1)).reshape(-1, degrees)
    products = [pltpu.VMEM((count, grid_count * channels, LANES), F32) for _, count in chunks]
    first = pl.pallas_call(
        functools.partial(first_body, dims, geometry),
        in_specs=[hbm] * 6,
        out_specs=[vmem] * (2 + len(chunks)),
        out_shape=[part, pltpu.VMEM((table_rows, columns), F32), *products],
        scratch_shapes=[
            pltpu.SMEM(l_atom.shape, jnp.int32),
            pltpu.SMEM(kgrid.shape, F32),
            pltpu.VMEM((1, ps_channels), jnp.int32),
            pltpu.VMEM(six.shape, F32),
            pltpu.VMEM((grid_count, channels, radial), BF16),
            pltpu.VMEM(ps_form.shape, BF16),
            pltpu.VMEM((levels, 2 * SUB * total_j, LANES), F32),
            pltpu.VMEM((degrees * grid_count, LANES), F32),
            pltpu.VMEM((table_rows, 2 * LANES), BF16),
            pltpu.SemaphoreType.DMA((5,)),
            pltpu.SemaphoreType.DMA((grid_count // BLOCK,)),
        ],
        compiler_params=params,
        name="first_half",
    )
    send, table, *products = first(
        *(
            pltpu.with_memory_space_constraint(x, pltpu.HBM)
            for x in (
                l_atom, kgrid, l_ps.reshape(1, -1), six, amplitude.reshape(grid_count, channels, radial), ps_form
            )
        )
    )
    other = lax.ppermute(send, "core", [(0, 1), (1, 0)])
    keep = pl.pallas_call(
        functools.partial(second_body, geometry),
        in_specs=[smem] + [vmem] * (1 + len(chunks)),
        out_specs=vmem,
        out_shape=part,
        compiler_params=params,
        name="second_half",
    )(l_atom, table, *products)
    mine = (keep + other).reshape(groups * total_j, tiles * owned, 1, LANES)
    got = lax.all_to_all(mine, ("zl", "x", "zh", "y"), split_axis=0, concat_axis=0, tiled=True)
    total = pl.pallas_call(
        functools.partial(sum_body, owned, tiles, groups, total_j),
        in_specs=[vmem],
        out_specs=vmem,
        out_shape=jax.ShapeDtypeStruct((owned, total_j, columns), F32),
        compiler_params=params,
        name="sum_sources",
    )(got.reshape(part.shape))
    return total[:, None]


def solution(mesh):
    fine = Mesh(mesh.devices.reshape(2, 4, 2, 2, 4), ("zl", "x", "core", "zh", "y"))
    ang, slab = ("zl", "x", "core"), ("zh", "y")
    in_specs = (P(ang, None, slab, None), P(), P(), P(), P(), P())
    out_specs = P(ang, slab, None, None)
    return jax.shard_map(local, mesh=fine, in_specs=in_specs, out_specs=out_specs, check_vma=False)
```

```python
import functools
import math

import jax
import jax.numpy as jnp
from jax import lax
from jax.experimental import pallas as pl
from jax.experimental.pallas import tpu as pltpu
from jax.sharding import Mesh, PartitionSpec as P

F32 = jnp.float32
BF16 = jnp.bfloat16
LANES = 128
SUB = 8
FIRST = 4
BLOCK = 8
VMEM_LIMIT = 28 * 1024 * 1024


def iota(shape, axis):
    return lax.broadcasted_iota(jnp.int32, shape, axis)


def build_tables(dims, place, kgrid, lps_ref, six_ref, r1_ref, pq_ref, x3_ref, w_ref):
    grid_count, total_points, degrees, levels, kpoints, ps_channels, columns = dims
    shape = (grid_count, LANES)
    position = (place[0] * grid_count + iota(shape, 0)).astype(F32)
    theta = math.pi * (position + 0.5) / total_points
    node = jnp.cos(theta)
    weight = (math.pi / total_points) * jnp.sin(theta)
    kidx = iota(shape, 1) % kpoints
    kcol = jnp.zeros(shape, F32)
    for q in range(kpoints):
        kcol = jnp.where(kidx == q, kgrid[q], kcol)
    krow = kgrid[place[1]]
    qinverse = 1.0 / (1.0 + krow * krow + kcol * kcol - 2.0 * node * krow * kcol)
    scale = weight * qinverse
    series = [jnp.ones(shape, F32), node]
    for degree in range(1, degrees - 1):
        series.append(((2 * degree + 1) * node * series[-1] - degree * series[-2]) / (degree + 1))
    for degree in range(degrees):
        pq_ref[pl.ds(degree * grid_count, grid_count), :] = series[degree] * scale
    half = levels * kpoints
    pad = 2 * SUB
    eye = (iota((pad, degrees), 0) == iota((pad, degrees), 1)).astype(F32)
    turned = lax.dot_general(
        eye, six_ref[...], (((1,), (1,)), ((), ())), precision=lax.Precision.HIGHEST, preferred_element_type=F32
    )
    pairs = levels * levels
    turned = jnp.concatenate([turned[:, j * pairs:(j + 1) * pairs] for j in range(SUB)], axis=0)
    spread_shape = (pairs, levels * LANES)
    source = iota(spread_shape, 0)
    target = iota(spread_shape, 1)
    wanted = (target // LANES) * levels + (target % half) // kpoints
    spread = (source == wanted).astype(F32)
    expanded = jnp.dot(turned, spread, precision=lax.Precision.HIGHEST, preferred_element_type=F32)
    for level in range(levels):
        r1_ref[level] = expanded[:, level * LANES:(level + 1) * LANES]
    low = iota((2 * SUB, LANES), 1) < half
    for level in range(levels):
        coef = [r1_ref[level, pl.ds(degree, SUB, stride=pad), :] for degree in range(degrees)]
        for pair in range(grid_count // 2):
            both = []
            for g in (2 * pair, 2 * pair + 1):
                acc = None
                for degree in range(degrees):
                    row = pq_ref[pl.ds(degree * grid_count + g, SUB, stride=0), :]
                    term = coef[degree] * row
                    acc = term if acc is None else acc + term
                both.append(acc)
            value = jnp.concatenate(both, axis=0)
            hi = value.astype(BF16).astype(F32)
            rest = value - hi
            mid = rest.astype(BF16).astype(F32)
            tail = rest - mid
            rows = pl.ds((level * grid_count + 2 * pair) * SUB, 2 * SUB)
            x3_ref[rows, 0:LANES] = jnp.where(low, hi, mid).astype(BF16)
            x3_ref[rows, LANES:2 * LANES] = jnp.where(low, tail, 0.0).astype(BF16)
    rep_shape = (ps_channels, columns)
    rep = (iota(rep_shape, 0) == iota(rep_shape, 1) // kpoints).astype(F32)
    level_of = jnp.dot(lps_ref[...].astype(F32), rep, preferred_element_type=F32)
    code = level_of.astype(jnp.int32) * kpoints + iota((1, columns), 1) % kpoints
    r = iota((2 * LANES, columns), 0)
    pick = ((r % half == code) & (r < 3 * half)).astype(F32).astype(BF16)
    w_ref[...] = jnp.dot(x3_ref[...], pick, preferred_element_type=F32)


def recouple(geometry, l_atom, i_ref, w_ref, out_ref, chunk, core):
    grid_count, channels, owned, groups, tiles = geometry
    first_tile, count = chunk
    rows, jump = (owned, groups * SUB * owned) if first_tile == 0 else (count * owned, owned)

    def group(d, carry):
        for r in range(owned):
            a = (2 * d + core) * owned + r
            base = l_atom[a] * (grid_count * SUB)
            acc = [None] * count
            for g in range(grid_count):
                for t in range(count):
                    lo = (first_tile + t) * LANES
                    coef = w_ref[pl.ds(pl.multiple_of(base + g * SUB, SUB), SUB), lo:lo + LANES]
                    term = coef * i_ref[t, pl.ds(g * channels + a, SUB, stride=0), :]
                    acc[t] = term if acc[t] is None else acc[t] + term
            for t in range(count):
                out_ref[pl.ds(d * (SUB * rows) + t * jump + r, SUB, stride=rows), :] = acc[t]
        return carry

    lax.fori_loop(0, groups, group, 0)


def multiply(geometry, a_ref, ps_ref, i_ref, chunk, before):
    grid_count, channels = geometry[:2]
    first_tile, count = chunk
    rows = BLOCK * channels

    def step(m, carry):
        before(m)
        left = a_ref[pl.ds(m * BLOCK, BLOCK)].reshape(rows, a_ref.shape[-1])
        right = ps_ref[:, first_tile * LANES:(first_tile + count) * LANES]
        product = jnp.dot(left, right, preferred_element_type=F32)
        for t in range(count):
            i_ref[t, pl.ds(pl.multiple_of(m * rows, rows), rows), :] = product[:, t * LANES:(t + 1) * LANES]
        return carry

    lax.fori_loop(0, grid_count // BLOCK, step, 0)


def first_body(dims, geometry, chunks, la_hbm, kg_hbm, lps_hbm, six_hbm, a_hbm, ps_hbm,
               send_ref, w_ref, i_ref, a_ref, ps_ref,
               l_atom, kgrid, lps_ref, six_ref, r1_ref, pq_ref, x3_ref, sems, a_sems):
    grid_count = geometry[0]
    core = lax.axis_index("core")
    ang = (lax.axis_index("zl") * lax.axis_size("x") + lax.axis_index("x")) * lax.axis_size("core") + core
    slab = lax.axis_index("zh") * lax.axis_size("y") + lax.axis_index("y")

    def copy_a(m):
        block = pl.ds(m * BLOCK, BLOCK)
        return pltpu.make_async_copy(a_hbm.at[block], a_ref.at[block], a_sems.at[m])

    columns = [pl.ds(tile * LANES, count * LANES) for tile, count in chunks]
    pairs = (
        (kg_hbm, kgrid), (six_hbm, six_ref), (lps_hbm, lps_ref), (la_hbm, l_atom),
        (ps_hbm.at[:, columns[0]], ps_ref.at[:, columns[0]]),
        (ps_hbm.at[:, columns[1]], ps_ref.at[:, columns[1]]),
    )
    copies = [pltpu.make_async_copy(source, target, sems.at[i]) for i, (source, target) in enumerate(pairs)]
    for copy in copies[:5]:
        copy.start()
    for m in range(grid_count // BLOCK):
        copy_a(m).start()
    copies[5].start()
    for copy in copies[:3]:
        copy.wait()
    build_tables(dims, (ang, slab), kgrid, lps_ref, six_ref, r1_ref, pq_ref, x3_ref, w_ref)
    for copy in copies[3:5]:
        copy.wait()
    multiply(geometry, a_ref, ps_ref, i_ref, chunks[0], lambda m: copy_a(m).wait())
    recouple(geometry, l_atom, i_ref, w_ref, send_ref, chunks[0], 1 - core)
    copies[5].wait()


def next_body(geometry, chunk, l_atom, w_ref, a_ref, ps_ref, gate, send_ref, keep_ref, i_ref):
    multiply(geometry, a_ref, ps_ref, i_ref, chunk, lambda m: None)
    core = lax.axis_index("core")
    recouple(geometry, l_atom, i_ref, w_ref, send_ref, chunk, 1 - core)
    recouple(geometry, l_atom, i_ref, w_ref, keep_ref, chunk, core)


def own_body(geometry, chunk, l_atom, w_ref, i_ref, keep_ref):
    recouple(geometry, l_atom, i_ref, w_ref, keep_ref, chunk, lax.axis_index("core"))


def split_body(rows, keep_ref, other_ref, z_keep_ref, z_send_ref, x_keep_ref, x_send_ref):
    z = lax.axis_index("zl")
    x = lax.axis_index("x") % 2
    for tile, out_ref in ((z, z_keep_ref), (1 - z, z_send_ref), (2 + x, x_keep_ref), (3 - x, x_send_ref)):
        at = pl.ds(pl.multiple_of(tile * rows, SUB), rows)
        out_ref[...] = keep_ref[at, :] + other_ref[at, :]


def join_body(owned, places, count, zk_ref, zo_ref, xk_ref, xo_ref, keep_ref, other_ref, out_ref,
              z_ref, x_ref, c_ref):
    z_ref[...] = zk_ref[...] + zo_ref[...]
    x_ref[...] = xk_ref[...] + xo_ref[...]
    c_ref[...] = keep_ref[...] + other_ref[...]
    rows = (count + 2) * owned

    def group(d, carry):
        for n, (ref, width) in enumerate(((z_ref, owned), (x_ref, owned), (c_ref, count * owned))):
            for r in range(width):
                part = ref[pl.ds(d * (SUB * width) + r, SUB, stride=width), :]
                out_ref[pl.ds(d * (SUB * rows) + n * owned + r, SUB, stride=rows), :] = part
        return carry

    lax.fori_loop(0, places // SUB, group, 0)


def sum_body(owned, sources, total_j, chunks, got_ref, out_ref):
    first, count = chunks[0][1], chunks[1][1]
    rows = (count + 2) * owned
    everyone = list(range(sources))
    half = sources // 2
    held = {0: (0, everyone[:half]), 1: (0, everyone[half:]), 2: (1, everyone[0::2]), 3: (1, everyone[1::2])}
    for t in range(count):
        held[first + t] = (2 + t, everyone)
    for r in range(owned):
        for t, (block, members) in held.items():
            acc = None
            for s in members:
                part = got_ref[pl.ds(s * total_j * rows + block * owned + r, total_j, stride=rows), :]
                acc = part if acc is None else acc + part
            out_ref[r, :, t * LANES:(t + 1) * LANES] = acc


def local(amplitude, ps_form, kgrid, l_atom, l_ps, sixj):
    grid_count, channels, slab_points, radial = amplitude.shape
    columns = ps_form.shape[1]
    kpoints = kgrid.shape[0]
    total_j, degrees, levels, _ = sixj.shape
    ps_channels = l_ps.shape[0]
    ang_size = lax.axis_size(("zl", "x", "core"))
    owned = channels // ang_size
    groups = ang_size // 2
    tiles = columns // LANES
    chunks = ((0, FIRST), (FIRST, tiles - FIRST))
    dims = (grid_count, grid_count * ang_size, degrees, levels, kpoints, ps_channels, columns)
    geometry = (grid_count, channels, owned, groups, tiles)
    smem = pl.BlockSpec(memory_space=pltpu.SMEM)
    vmem = pl.BlockSpec(memory_space=pltpu.VMEM)
    hbm = pl.BlockSpec(memory_space=pltpu.HBM)
    params = pltpu.CompilerParams(vmem_limit_bytes=VMEM_LIMIT)
    parts = [pltpu.VMEM((groups * total_j * count * owned, LANES), F32) for _, count in chunks]
    products = [pltpu.VMEM((count, grid_count * channels, LANES), F32) for _, count in chunks]
    table_rows = levels * grid_count * SUB
    six = jnp.transpose(sixj, (0, 2, 3, 1)).reshape(-1, degrees)
    inputs = (l_atom, kgrid, l_ps.reshape(1, -1), six, amplitude.reshape(grid_count, channels, radial), ps_form)
    send, table, product, left, right = pl.pallas_call(
        functools.partial(first_body, dims, geometry, chunks),
        in_specs=[hbm] * 6,
        out_specs=[vmem] * 5,
        out_shape=[
            parts[0],
            pltpu.VMEM((table_rows, columns), F32),
            products[0],
            pltpu.VMEM((grid_count, channels, radial), BF16),
            pltpu.VMEM(ps_form.shape, BF16),
        ],
        scratch_shapes=[
            pltpu.SMEM(l_atom.shape, jnp.int32),
            pltpu.SMEM(kgrid.shape, F32),
            pltpu.VMEM((1, ps_channels), jnp.int32),
            pltpu.VMEM(six.shape, F32),
            pltpu.VMEM((levels, 2 * SUB * total_j, LANES), F32),
            pltpu.VMEM((degrees * grid_count, LANES), F32),
            pltpu.VMEM((table_rows, 2 * LANES), BF16),
            pltpu.SemaphoreType.DMA((6,)),
            pltpu.SemaphoreType.DMA((grid_count // BLOCK,)),
        ],
        compiler_params=params,
        name="first_chunk",
    )(*(pltpu.with_memory_space_constraint(x, pltpu.HBM) for x in inputs))
    def own_part(n, product):
        return pl.pallas_call(
            functools.partial(own_body, geometry, chunks[n]),
            in_specs=[smem, vmem, vmem],
            out_specs=vmem,
            out_shape=parts[n],
            compiler_params=params,
            name="own_part",
        )(l_atom, table, product)

    places = groups * total_j
    swap = [(0, 1), (1, 0)]
    other = lax.ppermute(send, "core", swap)
    tile_part = pltpu.VMEM((places * owned, LANES), F32)
    z_keep, z_send, x_keep, x_send = pl.pallas_call(
        functools.partial(split_body, places * owned),
        in_specs=[vmem] * 2,
        out_specs=[vmem] * 4,
        out_shape=[tile_part] * 4,
        compiler_params=params,
        name="split_tiles",
    )(own_part(0, product), other)
    z_other = lax.ppermute(z_send, "zl", swap)
    x_other = lax.ppermute(x_send, "x", [(0, 1), (1, 0), (2, 3), (3, 2)])
    send, keep = pl.pallas_call(
        functools.partial(next_body, geometry, chunks[1]),
        in_specs=[smem, vmem, vmem, vmem, pl.BlockSpec(memory_space=pl.ANY)],
        out_specs=[vmem] * 2,
        out_shape=[parts[1]] * 2,
        scratch_shapes=[products[1]],
        compiler_params=params,
        name="next_chunk",
    )(l_atom, table, left, right, z_keep)
    send, z_other, x_other = lax.optimization_barrier((send, z_other, x_other))
    other = lax.ppermute(send, "core", swap)
    count = chunks[1][1]
    rows = (count + 2) * owned
    joined = pl.pallas_call(
        functools.partial(join_body, owned, places, count),
        in_specs=[vmem] * 6,
        out_specs=vmem,
        out_shape=pltpu.VMEM((places * rows, LANES), F32),
        scratch_shapes=[pltpu.VMEM((places * n * owned, LANES), F32) for n in (1, 1, count)],
        compiler_params=params,
        name="join_rows",
    )(z_keep, z_other, x_keep, x_other, keep, other)
    tile = joined.reshape(places, rows, 1, LANES)
    got = lax.all_to_all(tile, ("zl", "x", "zh", "y"), split_axis=0, concat_axis=0, tiled=True)
    total = pl.pallas_call(
        functools.partial(sum_body, owned, groups, total_j, chunks),
        in_specs=[vmem],
        out_specs=vmem,
        out_shape=jax.ShapeDtypeStruct((owned, total_j, columns), F32),
        compiler_params=params,
        name="sum_sources",
    )(got.reshape(-1, LANES))
    return total[:, None]


def solution(mesh):
    fine = Mesh(mesh.devices.reshape(2, 4, 2, 2, 4), ("zl", "x", "core", "zh", "y"))
    ang, slab = ("zl", "x", "core"), ("zh", "y")
    in_specs = (P(ang, None, slab, None), P(), P(), P(), P(), P())
    out_specs = P(ang, slab, None, None)
    return jax.shard_map(local, mesh=fine, in_specs=in_specs, out_specs=out_specs, check_vma=False)
```

```python
import functools
import math

import jax
import jax.numpy as jnp
from jax import lax
from jax.experimental import pallas as pl
from jax.experimental.pallas import tpu as pltpu
from jax.sharding import Mesh, PartitionSpec as P

F32 = jnp.float32
BF16 = jnp.bfloat16
LANES = 128
SUB = 8
FIRST = 4
BLOCK = 8
VMEM_LIMIT = 28 * 1024 * 1024


def iota(shape, axis):
    return lax.broadcasted_iota(jnp.int32, shape, axis)


def build_tables(dims, place, kgrid, lps_ref, six_ref, r1_ref, pq_ref, x3_ref, w_ref):
    grid_count, total_points, degrees, levels, kpoints, ps_channels, columns = dims
    shape = (grid_count, LANES)
    position = (place[0] * grid_count + iota(shape, 0)).astype(F32)
    theta = math.pi * (position + 0.5) / total_points
    node = jnp.cos(theta)
    weight = (math.pi / total_points) * jnp.sin(theta)
    kidx = iota(shape, 1) % kpoints
    kcol = jnp.zeros(shape, F32)
    for q in range(kpoints):
        kcol = jnp.where(kidx == q, kgrid[q], kcol)
    krow = kgrid[place[1]]
    qinverse = 1.0 / (1.0 + krow * krow + kcol * kcol - 2.0 * node * krow * kcol)
    scale = weight * qinverse
    series = [jnp.ones(shape, F32), node]
    for degree in range(1, degrees - 1):
        series.append(((2 * degree + 1) * node * series[-1] - degree * series[-2]) / (degree + 1))
    for degree in range(degrees):
        pq_ref[pl.ds(degree * grid_count, grid_count), :] = series[degree] * scale
    half = levels * kpoints
    pad = 2 * SUB
    eye = (iota((pad, degrees), 0) == iota((pad, degrees), 1)).astype(F32)
    turned = lax.dot_general(
        eye, six_ref[...], (((1,), (1,)), ((), ())), precision=lax.Precision.HIGHEST, preferred_element_type=F32
    )
    pairs = levels * levels
    turned = jnp.concatenate([turned[:, j * pairs:(j + 1) * pairs] for j in range(SUB)], axis=0)
    spread_shape = (pairs, levels * LANES)
    source = iota(spread_shape, 0)
    target = iota(spread_shape, 1)
    wanted = (target // LANES) * levels + (target % half) // kpoints
    spread = (source == wanted).astype(F32)
    expanded = jnp.dot(turned, spread, precision=lax.Precision.HIGHEST, preferred_element_type=F32)
    for level in range(levels):
        r1_ref[level] = expanded[:, level * LANES:(level + 1) * LANES]
    low = iota((2 * SUB, LANES), 1) < half
    for level in range(levels):
        coef = [r1_ref[level, pl.ds(degree, SUB, stride=pad), :] for degree in range(degrees)]
        for pair in range(grid_count // 2):
            both = []
            for g in (2 * pair, 2 * pair + 1):
                acc = None
                for degree in range(degrees):
                    row = pq_ref[pl.ds(degree * grid_count + g, SUB, stride=0), :]
                    term = coef[degree] * row
                    acc = term if acc is None else acc + term
                both.append(acc)
            value = jnp.concatenate(both, axis=0)
            hi = value.astype(BF16).astype(F32)
            rest = value - hi
            mid = rest.astype(BF16).astype(F32)
            tail = rest - mid
            rows = pl.ds((level * grid_count + 2 * pair) * SUB, 2 * SUB)
            x3_ref[rows, 0:LANES] = jnp.where(low, hi, mid).astype(BF16)
            x3_ref[rows, LANES:2 * LANES] = jnp.where(low, tail, 0.0).astype(BF16)
    rep_shape = (ps_channels, columns)
    rep = (iota(rep_shape, 0) == iota(rep_shape, 1) // kpoints).astype(F32)
    level_of = jnp.dot(lps_ref[...].astype(F32), rep, preferred_element_type=F32)
    code = level_of.astype(jnp.int32) * kpoints + iota((1, columns), 1) % kpoints
    r = iota((2 * LANES, columns), 0)
    pick = ((r % half == code) & (r < 3 * half)).astype(F32).astype(BF16)
    w_ref[...] = jnp.dot(x3_ref[...], pick, preferred_element_type=F32)


def recouple(geometry, l_atom, i_ref, w_ref, out_ref, chunk, core):
    grid_count, channels, owned, groups, tiles = geometry
    first_tile, count = chunk
    rows, jump = (owned, groups * SUB * owned) if first_tile == 0 else (count * owned, owned)

    def group(d, carry):
        for r in range(owned):
            a = (2 * d + core) * owned + r
            base = l_atom[a] * (grid_count * SUB)
            acc = [None] * count
            for g in range(grid_count):
                for t in range(count):
                    lo = (first_tile + t) * LANES
                    coef = w_ref[pl.ds(pl.multiple_of(base + g * SUB, SUB), SUB), lo:lo + LANES]
                    term = coef * i_ref[t, pl.ds(g * channels + a, SUB, stride=0), :]
                    acc[t] = term if acc[t] is None else acc[t] + term
            for t in range(count):
                out_ref[pl.ds(d * (SUB * rows) + t * jump + r, SUB, stride=rows), :] = acc[t]
        return carry

    lax.fori_loop(0, groups, group, 0)


def multiply(geometry, a_ref, ps_ref, i_ref, chunk, before):
    grid_count, channels = geometry[:2]
    first_tile, count = chunk
    rows = BLOCK * channels

    def step(m, carry):
        before(m)
        left = a_ref[pl.ds(m * BLOCK, BLOCK)].reshape(rows, a_ref.shape[-1])
        right = ps_ref[:, first_tile * LANES:(first_tile + count) * LANES]
        product = jnp.dot(left, right, preferred_element_type=F32)
        for t in range(count):
            i_ref[t, pl.ds(pl.multiple_of(m * rows, rows), rows), :] = product[:, t * LANES:(t + 1) * LANES]
        return carry

    lax.fori_loop(0, grid_count // BLOCK, step, 0)


def first_body(dims, geometry, chunks, la_hbm, kg_hbm, lps_hbm, six_hbm, a_hbm, ps_hbm,
               send_ref, w_ref, i_ref, a_ref, ps_ref,
               l_atom, kgrid, lps_ref, six_ref, r1_ref, pq_ref, x3_ref, sems, a_sems):
    grid_count = geometry[0]
    core = lax.axis_index("core")
    ang = (lax.axis_index("zl") * lax.axis_size("x") + lax.axis_index("x")) * lax.axis_size("core") + core
    slab = lax.axis_index("zh") * lax.axis_size("y") + lax.axis_index("y")

    def copy_a(m):
        block = pl.ds(m * BLOCK, BLOCK)
        return pltpu.make_async_copy(a_hbm.at[block], a_ref.at[block], a_sems.at[m])

    columns = [pl.ds(tile * LANES, count * LANES) for tile, count in chunks]
    pairs = (
        (kg_hbm, kgrid), (six_hbm, six_ref), (lps_hbm, lps_ref), (la_hbm, l_atom),
        (ps_hbm.at[:, columns[0]], ps_ref.at[:, columns[0]]),
        (ps_hbm.at[:, columns[1]], ps_ref.at[:, columns[1]]),
    )
    copies = [pltpu.make_async_copy(source, target, sems.at[i]) for i, (source, target) in enumerate(pairs)]
    for copy in copies[:5]:
        copy.start()
    for m in range(grid_count // BLOCK):
        copy_a(m).start()
    copies[5].start()
    for copy in copies[:3]:
        copy.wait()
    build_tables(dims, (ang, slab), kgrid, lps_ref, six_ref, r1_ref, pq_ref, x3_ref, w_ref)
    for copy in copies[3:5]:
        copy.wait()
    multiply(geometry, a_ref, ps_ref, i_ref, chunks[0], lambda m: copy_a(m).wait())
    recouple(geometry, l_atom, i_ref, w_ref, send_ref, chunks[0], 1 - core)
    copies[5].wait()


def next_body(geometry, chunk, l_atom, w_ref, a_ref, ps_ref, gate, send_ref, i_ref):
    multiply(geometry, a_ref, ps_ref, i_ref, chunk, lambda m: None)
    recouple(geometry, l_atom, i_ref, w_ref, send_ref, chunk, 1 - lax.axis_index("core"))


def own_body(geometry, chunk, l_atom, w_ref, i_ref, keep_ref):
    recouple(geometry, l_atom, i_ref, w_ref, keep_ref, chunk, lax.axis_index("core"))


def split_body(rows, keep_ref, other_ref, z_keep_ref, z_send_ref, x_keep_ref, x_send_ref):
    z = lax.axis_index("zl")
    x = lax.axis_index("x") % 2
    for tile, out_ref in ((z, z_keep_ref), (1 - z, z_send_ref), (2 + x, x_keep_ref), (3 - x, x_send_ref)):
        at = pl.ds(pl.multiple_of(tile * rows, SUB), rows)
        out_ref[...] = keep_ref[at, :] + other_ref[at, :]


def join_body(owned, places, count, zk_ref, zo_ref, xk_ref, xo_ref, keep_ref, other_ref, out_ref,
              z_ref, x_ref, c_ref):
    z_ref[...] = zk_ref[...] + zo_ref[...]
    x_ref[...] = xk_ref[...] + xo_ref[...]
    c_ref[...] = keep_ref[...] + other_ref[...]
    rows = (count + 2) * owned

    def group(d, carry):
        for n, (ref, width) in enumerate(((z_ref, owned), (x_ref, owned), (c_ref, count * owned))):
            for r in range(width):
                part = ref[pl.ds(d * (SUB * width) + r, SUB, stride=width), :]
                out_ref[pl.ds(d * (SUB * rows) + n * owned + r, SUB, stride=rows), :] = part
        return carry

    lax.fori_loop(0, places // SUB, group, 0)


def sum_body(owned, sources, total_j, chunks, got_ref, out_ref):
    first, count = chunks[0][1], chunks[1][1]
    rows = (count + 2) * owned
    everyone = list(range(sources))
    half = sources // 2
    held = {0: (0, everyone[:half]), 1: (0, everyone[half:]), 2: (1, everyone[0::2]), 3: (1, everyone[1::2])}
    for t in range(count):
        held[first + t] = (2 + t, everyone)
    for r in range(owned):
        for t, (block, members) in held.items():
            acc = None
            for s in members:
                part = got_ref[pl.ds(s * total_j * rows + block * owned + r, total_j, stride=rows), :]
                acc = part if acc is None else acc + part
            out_ref[r, :, t * LANES:(t + 1) * LANES] = acc


def local(amplitude, ps_form, kgrid, l_atom, l_ps, sixj):
    grid_count, channels, slab_points, radial = amplitude.shape
    columns = ps_form.shape[1]
    kpoints = kgrid.shape[0]
    total_j, degrees, levels, _ = sixj.shape
    ps_channels = l_ps.shape[0]
    ang_size = lax.axis_size(("zl", "x", "core"))
    owned = channels // ang_size
    groups = ang_size // 2
    tiles = columns // LANES
    chunks = ((0, FIRST), (FIRST, tiles - FIRST))
    dims = (grid_count, grid_count * ang_size, degrees, levels, kpoints, ps_channels, columns)
    geometry = (grid_count, channels, owned, groups, tiles)
    smem = pl.BlockSpec(memory_space=pltpu.SMEM)
    vmem = pl.BlockSpec(memory_space=pltpu.VMEM)
    hbm = pl.BlockSpec(memory_space=pltpu.HBM)
    params = pltpu.CompilerParams(vmem_limit_bytes=VMEM_LIMIT)
    parts = [pltpu.VMEM((groups * total_j * count * owned, LANES), F32) for _, count in chunks]
    products = [pltpu.VMEM((count, grid_count * channels, LANES), F32) for _, count in chunks]
    table_rows = levels * grid_count * SUB
    six = jnp.transpose(sixj, (0, 2, 3, 1)).reshape(-1, degrees)
    inputs = (l_atom, kgrid, l_ps.reshape(1, -1), six, amplitude.reshape(grid_count, channels, radial), ps_form)
    send, table, product, left, right = pl.pallas_call(
        functools.partial(first_body, dims, geometry, chunks),
        in_specs=[hbm] * 6,
        out_specs=[vmem] * 5,
        out_shape=[
            parts[0],
            pltpu.VMEM((table_rows, columns), F32),
            products[0],
            pltpu.VMEM((grid_count, channels, radial), BF16),
            pltpu.VMEM(ps_form.shape, BF16),
        ],
        scratch_shapes=[
            pltpu.SMEM(l_atom.shape, jnp.int32),
            pltpu.SMEM(kgrid.shape, F32),
            pltpu.VMEM((1, ps_channels), jnp.int32),
            pltpu.VMEM(six.shape, F32),
            pltpu.VMEM((levels, 2 * SUB * total_j, LANES), F32),
            pltpu.VMEM((degrees * grid_count, LANES), F32),
            pltpu.VMEM((table_rows, 2 * LANES), BF16),
            pltpu.SemaphoreType.DMA((6,)),
            pltpu.SemaphoreType.DMA((grid_count // BLOCK,)),
        ],
        compiler_params=params,
        name="first_chunk",
    )(*(pltpu.with_memory_space_constraint(x, pltpu.HBM) for x in inputs))
    def own_part(n, product):
        return pl.pallas_call(
            functools.partial(own_body, geometry, chunks[n]),
            in_specs=[smem, vmem, vmem],
            out_specs=vmem,
            out_shape=parts[n],
            compiler_params=params,
            name="own_part",
        )(l_atom, table, product)

    places = groups * total_j
    swap = [(0, 1), (1, 0)]
    other = lax.ppermute(send, "core", swap)
    tile_part = pltpu.VMEM((places * owned, LANES), F32)
    z_keep, z_send, x_keep, x_send = pl.pallas_call(
        functools.partial(split_body, places * owned),
        in_specs=[vmem] * 2,
        out_specs=[vmem] * 4,
        out_shape=[tile_part] * 4,
        compiler_params=params,
        name="split_tiles",
    )(own_part(0, product), other)
    z_other = lax.ppermute(z_send, "zl", swap)
    x_other = lax.ppermute(x_send, "x", [(0, 1), (1, 0), (2, 3), (3, 2)])
    send, product = pl.pallas_call(
        functools.partial(next_body, geometry, chunks[1]),
        in_specs=[smem, vmem, vmem, vmem, pl.BlockSpec(memory_space=pl.ANY)],
        out_specs=[vmem] * 2,
        out_shape=[parts[1], products[1]],
        compiler_params=params,
        name="next_chunk",
    )(l_atom, table, left, right, z_keep)
    send, product, z_other, x_other = lax.optimization_barrier((send, product, z_other, x_other))
    other = lax.ppermute(send, "core", swap)
    keep = own_part(1, product)
    count = chunks[1][1]
    rows = (count + 2) * owned
    joined = pl.pallas_call(
        functools.partial(join_body, owned, places, count),
        in_specs=[vmem] * 6,
        out_specs=vmem,
        out_shape=pltpu.VMEM((places * rows, LANES), F32),
        scratch_shapes=[pltpu.VMEM((places * n * owned, LANES), F32) for n in (1, 1, count)],
        compiler_params=params,
        name="join_rows",
    )(z_keep, z_other, x_keep, x_other, keep, other)
    tile = joined.reshape(places, rows, 1, LANES)
    got = lax.all_to_all(tile, ("zl", "x", "zh", "y"), split_axis=0, concat_axis=0, tiled=True)
    total = pl.pallas_call(
        functools.partial(sum_body, owned, groups, total_j, chunks),
        in_specs=[vmem],
        out_specs=vmem,
        out_shape=jax.ShapeDtypeStruct((owned, total_j, columns), F32),
        compiler_params=params,
        name="sum_sources",
    )(got.reshape(-1, LANES))
    return total[:, None]


def solution(mesh):
    fine = Mesh(mesh.devices.reshape(2, 4, 2, 2, 4), ("zl", "x", "core", "zh", "y"))
    ang, slab = ("zl", "x", "core"), ("zh", "y")
    in_specs = (P(ang, None, slab, None), P(), P(), P(), P(), P())
    out_specs = P(ang, slab, None, None)
    return jax.shard_map(local, mesh=fine, in_specs=in_specs, out_specs=out_specs, check_vma=False)
```

```python
import functools
import math

import jax
import jax.numpy as jnp
from jax import lax
from jax.experimental import pallas as pl
from jax.experimental.pallas import tpu as pltpu
from jax.sharding import Mesh, PartitionSpec as P

F32 = jnp.float32
BF16 = jnp.bfloat16
LANES = 128
SUB = 8
FIRST = 6
BLOCK = 8
VMEM_LIMIT = 28 * 1024 * 1024


def iota(shape, axis):
    return lax.broadcasted_iota(jnp.int32, shape, axis)


def build_tables(dims, place, kgrid, lps_ref, six_ref, r1_ref, pq_ref, x3_ref, w_ref):
    grid_count, total_points, degrees, levels, kpoints, ps_channels, columns = dims
    shape = (grid_count, LANES)
    position = (place[0] * grid_count + iota(shape, 0)).astype(F32)
    theta = math.pi * (position + 0.5) / total_points
    node = jnp.cos(theta)
    weight = (math.pi / total_points) * jnp.sin(theta)
    kidx = iota(shape, 1) % kpoints
    kcol = jnp.zeros(shape, F32)
    for q in range(kpoints):
        kcol = jnp.where(kidx == q, kgrid[q], kcol)
    krow = kgrid[place[1]]
    qinverse = 1.0 / (1.0 + krow * krow + kcol * kcol - 2.0 * node * krow * kcol)
    scale = weight * qinverse
    series = [jnp.ones(shape, F32), node]
    for degree in range(1, degrees - 1):
        series.append(((2 * degree + 1) * node * series[-1] - degree * series[-2]) / (degree + 1))
    for degree in range(degrees):
        pq_ref[pl.ds(degree * grid_count, grid_count), :] = series[degree] * scale
    half = levels * kpoints
    pad = 2 * SUB
    eye = (iota((pad, degrees), 0) == iota((pad, degrees), 1)).astype(F32)
    turned = lax.dot_general(
        eye, six_ref[...], (((1,), (1,)), ((), ())), precision=lax.Precision.HIGHEST, preferred_element_type=F32
    )
    pairs = levels * levels
    turned = jnp.concatenate([turned[:, j * pairs:(j + 1) * pairs] for j in range(SUB)], axis=0)
    spread_shape = (pairs, levels * LANES)
    source = iota(spread_shape, 0)
    target = iota(spread_shape, 1)
    wanted = (target // LANES) * levels + (target % half) // kpoints
    spread = (source == wanted).astype(F32)
    expanded = jnp.dot(turned, spread, precision=lax.Precision.HIGHEST, preferred_element_type=F32)
    for level in range(levels):
        r1_ref[level] = expanded[:, level * LANES:(level + 1) * LANES]
    low = iota((2 * SUB, LANES), 1) < half
    for level in range(levels):
        coef = [r1_ref[level, pl.ds(degree, SUB, stride=pad), :] for degree in range(degrees)]
        for pair in range(grid_count // 2):
            both = []
            for g in (2 * pair, 2 * pair + 1):
                acc = None
                for degree in range(degrees):
                    row = pq_ref[pl.ds(degree * grid_count + g, SUB, stride=0), :]
                    term = coef[degree] * row
                    acc = term if acc is None else acc + term
                both.append(acc)
            value = jnp.concatenate(both, axis=0)
            hi = value.astype(BF16).astype(F32)
            rest = value - hi
            mid = rest.astype(BF16).astype(F32)
            tail = rest - mid
            rows = pl.ds((level * grid_count + 2 * pair) * SUB, 2 * SUB)
            x3_ref[rows, 0:LANES] = jnp.where(low, hi, mid).astype(BF16)
            x3_ref[rows, LANES:2 * LANES] = jnp.where(low, tail, 0.0).astype(BF16)
    rep_shape = (ps_channels, columns)
    rep = (iota(rep_shape, 0) == iota(rep_shape, 1) // kpoints).astype(F32)
    level_of = jnp.dot(lps_ref[...].astype(F32), rep, preferred_element_type=F32)
    code = level_of.astype(jnp.int32) * kpoints + iota((1, columns), 1) % kpoints
    r = iota((2 * LANES, columns), 0)
    pick = ((r % half == code) & (r < 3 * half)).astype(F32).astype(BF16)
    w_ref[...] = jnp.dot(x3_ref[...], pick, preferred_element_type=F32)


def recouple(geometry, l_atom, i_ref, w_ref, out_ref, chunk, core):
    grid_count, channels, owned, groups, tiles = geometry
    first_tile, count = chunk
    rows, jump = (owned, groups * SUB * owned) if first_tile == 0 else (count * owned, owned)

    def group(d, carry):
        for r in range(owned):
            a = (2 * d + core) * owned + r
            base = l_atom[a] * (grid_count * SUB)
            acc = [None] * count
            for g in range(grid_count):
                for t in range(count):
                    lo = (first_tile + t) * LANES
                    coef = w_ref[pl.ds(pl.multiple_of(base + g * SUB, SUB), SUB), lo:lo + LANES]
                    term = coef * i_ref[t, pl.ds(g * channels + a, SUB, stride=0), :]
                    acc[t] = term if acc[t] is None else acc[t] + term
            for t in range(count):
                out_ref[pl.ds(d * (SUB * rows) + t * jump + r, SUB, stride=rows), :] = acc[t]
        return carry

    lax.fori_loop(0, groups, group, 0)


def multiply(geometry, a_ref, ps_ref, i_ref, chunk, before):
    grid_count, channels = geometry[:2]
    first_tile, count = chunk
    rows = BLOCK * channels

    def step(m, carry):
        before(m)
        left = a_ref[pl.ds(m * BLOCK, BLOCK)].reshape(rows, a_ref.shape[-1])
        right = ps_ref[:, first_tile * LANES:(first_tile + count) * LANES]
        product = jnp.dot(left, right, preferred_element_type=F32)
        for t in range(count):
            i_ref[t, pl.ds(pl.multiple_of(m * rows, rows), rows), :] = product[:, t * LANES:(t + 1) * LANES]
        return carry

    lax.fori_loop(0, grid_count // BLOCK, step, 0)


def first_body(dims, geometry, chunks, la_hbm, kg_hbm, lps_hbm, six_hbm, a_hbm, ps_hbm,
               send_ref, w_ref, i_ref, a_ref, ps_ref,
               l_atom, kgrid, lps_ref, six_ref, r1_ref, pq_ref, x3_ref, sems, a_sems):
    grid_count = geometry[0]
    core = lax.axis_index("core")
    ang = (lax.axis_index("zl") * lax.axis_size("x") + lax.axis_index("x")) * lax.axis_size("core") + core
    slab = lax.axis_index("zh") * lax.axis_size("y") + lax.axis_index("y")

    def copy_a(m):
        block = pl.ds(m * BLOCK, BLOCK)
        return pltpu.make_async_copy(a_hbm.at[block], a_ref.at[block], a_sems.at[m])

    columns = [pl.ds(tile * LANES, count * LANES) for tile, count in chunks]
    pairs = (
        (kg_hbm, kgrid), (six_hbm, six_ref), (lps_hbm, lps_ref), (la_hbm, l_atom),
        (ps_hbm.at[:, columns[0]], ps_ref.at[:, columns[0]]),
        (ps_hbm.at[:, columns[1]], ps_ref.at[:, columns[1]]),
    )
    copies = [pltpu.make_async_copy(source, target, sems.at[i]) for i, (source, target) in enumerate(pairs)]
    for copy in copies[:5]:
        copy.start()
    for m in range(grid_count // BLOCK):
        copy_a(m).start()
    copies[5].start()
    for copy in copies[:3]:
        copy.wait()
    build_tables(dims, (ang, slab), kgrid, lps_ref, six_ref, r1_ref, pq_ref, x3_ref, w_ref)
    for copy in copies[3:5]:
        copy.wait()
    multiply(geometry, a_ref, ps_ref, i_ref, chunks[0], lambda m: copy_a(m).wait())
    recouple(geometry, l_atom, i_ref, w_ref, send_ref, chunks[0], 1 - core)
    copies[5].wait()


def next_body(geometry, chunk, l_atom, w_ref, a_ref, ps_ref, gate, send_ref, i_ref):
    multiply(geometry, a_ref, ps_ref, i_ref, chunk, lambda m: None)
    recouple(geometry, l_atom, i_ref, w_ref, send_ref, chunk, 1 - lax.axis_index("core"))


def own_body(geometry, chunk, l_atom, w_ref, i_ref, keep_ref):
    recouple(geometry, l_atom, i_ref, w_ref, keep_ref, chunk, lax.axis_index("core"))


def split_body(rows, keep_ref, other_ref, z_keep_ref, z_send_ref, x_keep_ref, x_send_ref, y_keep_ref, y_send_ref):
    z = lax.axis_index("zl")
    x = lax.axis_index("x") % 2
    y = (lax.axis_index("x") + 1) % 2
    for tile, out_ref in (
        (z, z_keep_ref), (1 - z, z_send_ref), (2 + x, x_keep_ref), (3 - x, x_send_ref),
        (4 + y, y_keep_ref), (5 - y, y_send_ref),
    ):
        at = pl.ds(pl.multiple_of(tile * rows, SUB), rows)
        out_ref[...] = keep_ref[at, :] + other_ref[at, :]


def join_body(owned, places, count, zk_ref, zo_ref, xk_ref, xo_ref, yk_ref, yo_ref, keep_ref, other_ref, out_ref,
              z_ref, x_ref, y_ref, c_ref):
    z_ref[...] = zk_ref[...] + zo_ref[...]
    x_ref[...] = xk_ref[...] + xo_ref[...]
    y_ref[...] = yk_ref[...] + yo_ref[...]
    c_ref[...] = keep_ref[...] + other_ref[...]
    rows = (count + 3) * owned

    def group(d, carry):
        for n, (ref, width) in enumerate(((z_ref, owned), (x_ref, owned), (y_ref, owned), (c_ref, count * owned))):
            for r in range(width):
                part = ref[pl.ds(d * (SUB * width) + r, SUB, stride=width), :]
                out_ref[pl.ds(d * (SUB * rows) + n * owned + r, SUB, stride=rows), :] = part
        return carry

    lax.fori_loop(0, places // SUB, group, 0)


def sum_body(owned, sources, total_j, chunks, got_ref, out_ref):
    first, count = chunks[0][1], chunks[1][1]
    rows = (count + 3) * owned
    everyone = list(range(sources))
    half = sources // 2
    held = {0: (0, everyone[:half]), 1: (0, everyone[half:]), 2: (1, everyone[0::2]), 3: (1, everyone[1::2]),
            4: (2, everyone[1::2]), 5: (2, everyone[0::2])}
    for t in range(count):
        held[first + t] = (3 + t, everyone)
    for r in range(owned):
        for t, (block, members) in held.items():
            acc = None
            for s in members:
                part = got_ref[pl.ds(s * total_j * rows + block * owned + r, total_j, stride=rows), :]
                acc = part if acc is None else acc + part
            out_ref[r, :, t * LANES:(t + 1) * LANES] = acc


def local(amplitude, ps_form, kgrid, l_atom, l_ps, sixj):
    grid_count, channels, slab_points, radial = amplitude.shape
    columns = ps_form.shape[1]
    kpoints = kgrid.shape[0]
    total_j, degrees, levels, _ = sixj.shape
    ps_channels = l_ps.shape[0]
    ang_size = lax.axis_size(("zl", "x", "core"))
    owned = channels // ang_size
    groups = ang_size // 2
    tiles = columns // LANES
    chunks = ((0, FIRST), (FIRST, tiles - FIRST))
    dims = (grid_count, grid_count * ang_size, degrees, levels, kpoints, ps_channels, columns)
    geometry = (grid_count, channels, owned, groups, tiles)
    smem = pl.BlockSpec(memory_space=pltpu.SMEM)
    vmem = pl.BlockSpec(memory_space=pltpu.VMEM)
    hbm = pl.BlockSpec(memory_space=pltpu.HBM)
    params = pltpu.CompilerParams(vmem_limit_bytes=VMEM_LIMIT)
    parts = [pltpu.VMEM((groups * total_j * count * owned, LANES), F32) for _, count in chunks]
    products = [pltpu.VMEM((count, grid_count * channels, LANES), F32) for _, count in chunks]
    table_rows = levels * grid_count * SUB
    six = jnp.transpose(sixj, (0, 2, 3, 1)).reshape(-1, degrees)
    inputs = (l_atom, kgrid, l_ps.reshape(1, -1), six, amplitude.reshape(grid_count, channels, radial), ps_form)
    send, table, product, left, right = pl.pallas_call(
        functools.partial(first_body, dims, geometry, chunks),
        in_specs=[hbm] * 6,
        out_specs=[vmem] * 5,
        out_shape=[
            parts[0],
            pltpu.VMEM((table_rows, columns), F32),
            products[0],
            pltpu.VMEM((grid_count, channels, radial), BF16),
            pltpu.VMEM(ps_form.shape, BF16),
        ],
        scratch_shapes=[
            pltpu.SMEM(l_atom.shape, jnp.int32),
            pltpu.SMEM(kgrid.shape, F32),
            pltpu.VMEM((1, ps_channels), jnp.int32),
            pltpu.VMEM(six.shape, F32),
            pltpu.VMEM((levels, 2 * SUB * total_j, LANES), F32),
            pltpu.VMEM((degrees * grid_count, LANES), F32),
            pltpu.VMEM((table_rows, 2 * LANES), BF16),
            pltpu.SemaphoreType.DMA((6,)),
            pltpu.SemaphoreType.DMA((grid_count // BLOCK,)),
        ],
        compiler_params=params,
        name="first_chunk",
    )(*(pltpu.with_memory_space_constraint(x, pltpu.HBM) for x in inputs))
    def own_part(n, product):
        return pl.pallas_call(
            functools.partial(own_body, geometry, chunks[n]),
            in_specs=[smem, vmem, vmem],
            out_specs=vmem,
            out_shape=parts[n],
            compiler_params=params,
            name="own_part",
        )(l_atom, table, product)

    places = groups * total_j
    swap = [(0, 1), (1, 0)]
    other = lax.ppermute(send, "core", swap)
    tile_part = pltpu.VMEM((places * owned, LANES), F32)
    z_keep, z_send, x_keep, x_send, y_keep, y_send = pl.pallas_call(
        functools.partial(split_body, places * owned),
        in_specs=[vmem] * 2,
        out_specs=[vmem] * 6,
        out_shape=[tile_part] * 6,
        compiler_params=params,
        name="split_tiles",
    )(own_part(0, product), other)
    z_other = lax.ppermute(z_send, "zl", swap)
    x_other = lax.ppermute(x_send, "x", [(0, 1), (1, 0), (2, 3), (3, 2)])
    y_other = lax.ppermute(y_send, "x", [(0, 3), (3, 0), (1, 2), (2, 1)])
    send, product = pl.pallas_call(
        functools.partial(next_body, geometry, chunks[1]),
        in_specs=[smem, vmem, vmem, vmem, pl.BlockSpec(memory_space=pl.ANY)],
        out_specs=[vmem] * 2,
        out_shape=[parts[1], products[1]],
        compiler_params=params,
        name="next_chunk",
    )(l_atom, table, left, right, z_keep)
    send, product, z_other, x_other, y_other = lax.optimization_barrier((send, product, z_other, x_other, y_other))
    other = lax.ppermute(send, "core", swap)
    keep = own_part(1, product)
    count = chunks[1][1]
    rows = (count + 3) * owned
    joined = pl.pallas_call(
        functools.partial(join_body, owned, places, count),
        in_specs=[vmem] * 8,
        out_specs=vmem,
        out_shape=pltpu.VMEM((places * rows, LANES), F32),
        scratch_shapes=[pltpu.VMEM((places * n * owned, LANES), F32) for n in (1, 1, 1, count)],
        compiler_params=params,
        name="join_rows",
    )(z_keep, z_other, x_keep, x_other, y_keep, y_other, keep, other)
    tile = joined.reshape(places, rows, 1, LANES)
    got = lax.all_to_all(tile, ("zl", "x", "zh", "y"), split_axis=0, concat_axis=0, tiled=True)
    total = pl.pallas_call(
        functools.partial(sum_body, owned, groups, total_j, chunks),
        in_specs=[vmem],
        out_specs=vmem,
        out_shape=jax.ShapeDtypeStruct((owned, total_j, columns), F32),
        compiler_params=params,
        name="sum_sources",
    )(got.reshape(-1, LANES))
    return total[:, None]


def solution(mesh):
    fine = Mesh(mesh.devices.reshape(2, 4, 2, 2, 4), ("zl", "x", "core", "zh", "y"))
    ang, slab = ("zl", "x", "core"), ("zh", "y")
    in_specs = (P(ang, None, slab, None), P(), P(), P(), P(), P())
    out_specs = P(ang, slab, None, None)
    return jax.shard_map(local, mesh=fine, in_specs=in_specs, out_specs=out_specs, check_vma=False)
```

```python
import functools
import math

import jax
import jax.numpy as jnp
from jax import lax
from jax.experimental import pallas as pl
from jax.experimental.pallas import tpu as pltpu
from jax.sharding import Mesh, PartitionSpec as P

F32 = jnp.float32
BF16 = jnp.bfloat16
LANES = 128
SUB = 8
FIRST = 2
BLOCK = 8
VMEM_LIMIT = 28 * 1024 * 1024


def iota(shape, axis):
    return lax.broadcasted_iota(jnp.int32, shape, axis)


def build_tables(dims, place, kgrid, lps_ref, six_ref, r1_ref, pq_ref, x3_ref, w_ref):
    grid_count, total_points, degrees, levels, kpoints, ps_channels, columns = dims
    shape = (grid_count, LANES)
    position = (place[0] * grid_count + iota(shape, 0)).astype(F32)
    theta = math.pi * (position + 0.5) / total_points
    node = jnp.cos(theta)
    weight = (math.pi / total_points) * jnp.sin(theta)
    kidx = iota(shape, 1) % kpoints
    kcol = jnp.zeros(shape, F32)
    for q in range(kpoints):
        kcol = jnp.where(kidx == q, kgrid[q], kcol)
    krow = kgrid[place[1]]
    qinverse = 1.0 / (1.0 + krow * krow + kcol * kcol - 2.0 * node * krow * kcol)
    scale = weight * qinverse
    series = [jnp.ones(shape, F32), node]
    for degree in range(1, degrees - 1):
        series.append(((2 * degree + 1) * node * series[-1] - degree * series[-2]) / (degree + 1))
    for degree in range(degrees):
        pq_ref[pl.ds(degree * grid_count, grid_count), :] = series[degree] * scale
    half = levels * kpoints
    pad = 2 * SUB
    eye = (iota((pad, degrees), 0) == iota((pad, degrees), 1)).astype(F32)
    turned = lax.dot_general(
        eye, six_ref[...], (((1,), (1,)), ((), ())), precision=lax.Precision.HIGHEST, preferred_element_type=F32
    )
    pairs = levels * levels
    turned = jnp.concatenate([turned[:, j * pairs:(j + 1) * pairs] for j in range(SUB)], axis=0)
    spread_shape = (pairs, levels * LANES)
    source = iota(spread_shape, 0)
    target = iota(spread_shape, 1)
    wanted = (target // LANES) * levels + (target % half) // kpoints
    spread = (source == wanted).astype(F32)
    expanded = jnp.dot(turned, spread, precision=lax.Precision.HIGHEST, preferred_element_type=F32)
    for level in range(levels):
        r1_ref[level] = expanded[:, level * LANES:(level + 1) * LANES]
    low = iota((2 * SUB, LANES), 1) < half
    for level in range(levels):
        coef = [r1_ref[level, pl.ds(degree, SUB, stride=pad), :] for degree in range(degrees)]
        for pair in range(grid_count // 2):
            both = []
            for g in (2 * pair, 2 * pair + 1):
                acc = None
                for degree in range(degrees):
                    row = pq_ref[pl.ds(degree * grid_count + g, SUB, stride=0), :]
                    term = coef[degree] * row
                    acc = term if acc is None else acc + term
                both.append(acc)
            value = jnp.concatenate(both, axis=0)
            hi = value.astype(BF16).astype(F32)
            rest = value - hi
            mid = rest.astype(BF16).astype(F32)
            tail = rest - mid
            rows = pl.ds((level * grid_count + 2 * pair) * SUB, 2 * SUB)
            x3_ref[rows, 0:LANES] = jnp.where(low, hi, mid).astype(BF16)
            x3_ref[rows, LANES:2 * LANES] = jnp.where(low, tail, 0.0).astype(BF16)
    rep_shape = (ps_channels, columns)
    rep = (iota(rep_shape, 0) == iota(rep_shape, 1) // kpoints).astype(F32)
    level_of = jnp.dot(lps_ref[...].astype(F32), rep, preferred_element_type=F32)
    code = level_of.astype(jnp.int32) * kpoints + iota((1, columns), 1) % kpoints
    r = iota((2 * LANES, columns), 0)
    pick = ((r % half == code) & (r < 3 * half)).astype(F32).astype(BF16)
    w_ref[...] = jnp.dot(x3_ref[...], pick, preferred_element_type=F32)


def recouple(geometry, l_atom, i_ref, w_ref, out_ref, chunk, core):
    grid_count, channels, owned, groups, tiles = geometry
    first_tile, count = chunk
    rows, jump = (owned, groups * SUB * owned) if first_tile == 0 else (count * owned, owned)

    def group(d, carry):
        for r in range(owned):
            a = (2 * d + core) * owned + r
            base = l_atom[a] * (grid_count * SUB)
            acc = [None] * count
            for g in range(grid_count):
                for t in range(count):
                    lo = (first_tile + t) * LANES
                    coef = w_ref[pl.ds(pl.multiple_of(base + g * SUB, SUB), SUB), lo:lo + LANES]
                    term = coef * i_ref[t, pl.ds(g * channels + a, SUB, stride=0), :]
                    acc[t] = term if acc[t] is None else acc[t] + term
            for t in range(count):
                out_ref[pl.ds(d * (SUB * rows) + t * jump + r, SUB, stride=rows), :] = acc[t]
        return carry

    lax.fori_loop(0, groups, group, 0)


def multiply(geometry, a_ref, ps_ref, i_ref, chunk, before):
    grid_count, channels = geometry[:2]
    first_tile, count = chunk
    rows = BLOCK * channels

    def step(m, carry):
        before(m)
        left = a_ref[pl.ds(m * BLOCK, BLOCK)].reshape(rows, a_ref.shape[-1])
        right = ps_ref[:, first_tile * LANES:(first_tile + count) * LANES]
        product = jnp.dot(left, right, preferred_element_type=F32)
        for t in range(count):
            i_ref[t, pl.ds(pl.multiple_of(m * rows, rows), rows), :] = product[:, t * LANES:(t + 1) * LANES]
        return carry

    lax.fori_loop(0, grid_count // BLOCK, step, 0)


def first_body(dims, geometry, chunks, la_hbm, kg_hbm, lps_hbm, six_hbm, a_hbm, ps_hbm,
               send_ref, w_ref, i_ref, a_ref, ps_ref,
               l_atom, kgrid, lps_ref, six_ref, r1_ref, pq_ref, x3_ref, sems, a_sems):
    grid_count = geometry[0]
    core = lax.axis_index("core")
    ang = (lax.axis_index("zl") * lax.axis_size("x") + lax.axis_index("x")) * lax.axis_size("core") + core
    slab = lax.axis_index("zh") * lax.axis_size("y") + lax.axis_index("y")

    def copy_a(m):
        block = pl.ds(m * BLOCK, BLOCK)
        return pltpu.make_async_copy(a_hbm.at[block], a_ref.at[block], a_sems.at[m])

    columns = [pl.ds(tile * LANES, count * LANES) for tile, count in chunks]
    pairs = (
        (kg_hbm, kgrid), (six_hbm, six_ref), (lps_hbm, lps_ref), (la_hbm, l_atom),
        (ps_hbm.at[:, columns[0]], ps_ref.at[:, columns[0]]),
        (ps_hbm.at[:, columns[1]], ps_ref.at[:, columns[1]]),
    )
    copies = [pltpu.make_async_copy(source, target, sems.at[i]) for i, (source, target) in enumerate(pairs)]
    for copy in copies[:5]:
        copy.start()
    for m in range(grid_count // BLOCK):
        copy_a(m).start()
    copies[5].start()
    for copy in copies[:3]:
        copy.wait()
    build_tables(dims, (ang, slab), kgrid, lps_ref, six_ref, r1_ref, pq_ref, x3_ref, w_ref)
    for copy in copies[3:5]:
        copy.wait()
    multiply(geometry, a_ref, ps_ref, i_ref, chunks[0], lambda m: copy_a(m).wait())
    recouple(geometry, l_atom, i_ref, w_ref, send_ref, chunks[0], 1 - core)
    copies[5].wait()


def next_body(geometry, chunk, l_atom, w_ref, a_ref, ps_ref, gate, send_ref, i_ref):
    multiply(geometry, a_ref, ps_ref, i_ref, chunk, lambda m: None)
    recouple(geometry, l_atom, i_ref, w_ref, send_ref, chunk, 1 - lax.axis_index("core"))


def own_body(geometry, chunk, l_atom, w_ref, i_ref, keep_ref):
    recouple(geometry, l_atom, i_ref, w_ref, keep_ref, chunk, lax.axis_index("core"))


def split_body(rows, keep_ref, other_ref, z_keep_ref, z_send_ref):
    z = lax.axis_index("zl")
    for tile, out_ref in ((z, z_keep_ref), (1 - z, z_send_ref)):
        at = pl.ds(pl.multiple_of(tile * rows, SUB), rows)
        out_ref[...] = keep_ref[at, :] + other_ref[at, :]


def join_body(owned, places, count, zk_ref, zo_ref, keep_ref, other_ref, out_ref, z_ref, c_ref):
    z_ref[...] = zk_ref[...] + zo_ref[...]
    c_ref[...] = keep_ref[...] + other_ref[...]
    rows = (count + 1) * owned

    def group(d, carry):
        for n, (ref, width) in enumerate(((z_ref, owned), (c_ref, count * owned))):
            for r in range(width):
                part = ref[pl.ds(d * (SUB * width) + r, SUB, stride=width), :]
                out_ref[pl.ds(d * (SUB * rows) + n * owned + r, SUB, stride=rows), :] = part
        return carry

    lax.fori_loop(0, places // SUB, group, 0)


def sum_body(owned, sources, total_j, chunks, got_ref, out_ref):
    first, count = chunks[0][1], chunks[1][1]
    rows = (count + 1) * owned
    everyone = list(range(sources))
    half = sources // 2
    held = {0: (0, everyone[:half]), 1: (0, everyone[half:])}
    for t in range(count):
        held[first + t] = (1 + t, everyone)
    for r in range(owned):
        for t, (block, members) in held.items():
            acc = None
            for s in members:
                part = got_ref[pl.ds(s * total_j * rows + block * owned + r, total_j, stride=rows), :]
                acc = part if acc is None else acc + part
            out_ref[r, :, t * LANES:(t + 1) * LANES] = acc


def local(amplitude, ps_form, kgrid, l_atom, l_ps, sixj):
    grid_count, channels, slab_points, radial = amplitude.shape
    columns = ps_form.shape[1]
    kpoints = kgrid.shape[0]
    total_j, degrees, levels, _ = sixj.shape
    ps_channels = l_ps.shape[0]
    ang_size = lax.axis_size(("zl", "x", "core"))
    owned = channels // ang_size
    groups = ang_size // 2
    tiles = columns // LANES
    chunks = ((0, FIRST), (FIRST, tiles - FIRST))
    dims = (grid_count, grid_count * ang_size, degrees, levels, kpoints, ps_channels, columns)
    geometry = (grid_count, channels, owned, groups, tiles)
    smem = pl.BlockSpec(memory_space=pltpu.SMEM)
    vmem = pl.BlockSpec(memory_space=pltpu.VMEM)
    hbm = pl.BlockSpec(memory_space=pltpu.HBM)
    params = pltpu.CompilerParams(vmem_limit_bytes=VMEM_LIMIT)
    parts = [pltpu.VMEM((groups * total_j * count * owned, LANES), F32) for _, count in chunks]
    products = [pltpu.VMEM((count, grid_count * channels, LANES), F32) for _, count in chunks]
    table_rows = levels * grid_count * SUB
    six = jnp.transpose(sixj, (0, 2, 3, 1)).reshape(-1, degrees)
    inputs = (l_atom, kgrid, l_ps.reshape(1, -1), six, amplitude.reshape(grid_count, channels, radial), ps_form)
    send, table, product, left, right = pl.pallas_call(
        functools.partial(first_body, dims, geometry, chunks),
        in_specs=[hbm] * 6,
        out_specs=[vmem] * 5,
        out_shape=[
            parts[0],
            pltpu.VMEM((table_rows, columns), F32),
            products[0],
            pltpu.VMEM((grid_count, channels, radial), BF16),
            pltpu.VMEM(ps_form.shape, BF16),
        ],
        scratch_shapes=[
            pltpu.SMEM(l_atom.shape, jnp.int32),
            pltpu.SMEM(kgrid.shape, F32),
            pltpu.VMEM((1, ps_channels), jnp.int32),
            pltpu.VMEM(six.shape, F32),
            pltpu.VMEM((levels, 2 * SUB * total_j, LANES), F32),
            pltpu.VMEM((degrees * grid_count, LANES), F32),
            pltpu.VMEM((table_rows, 2 * LANES), BF16),
            pltpu.SemaphoreType.DMA((6,)),
            pltpu.SemaphoreType.DMA((grid_count // BLOCK,)),
        ],
        compiler_params=params,
        name="first_chunk",
    )(*(pltpu.with_memory_space_constraint(x, pltpu.HBM) for x in inputs))
    def own_part(n, product):
        return pl.pallas_call(
            functools.partial(own_body, geometry, chunks[n]),
            in_specs=[smem, vmem, vmem],
            out_specs=vmem,
            out_shape=parts[n],
            compiler_params=params,
            name="own_part",
        )(l_atom, table, product)

    places = groups * total_j
    swap = [(0, 1), (1, 0)]
    other = lax.ppermute(send, "core", swap)
    tile_part = pltpu.VMEM((places * owned, LANES), F32)
    z_keep, z_send = pl.pallas_call(
        functools.partial(split_body, places * owned),
        in_specs=[vmem] * 2,
        out_specs=[vmem] * 2,
        out_shape=[tile_part] * 2,
        compiler_params=params,
        name="split_tiles",
    )(own_part(0, product), other)
    z_other = lax.ppermute(z_send, "zl", swap)
    send, product = pl.pallas_call(
        functools.partial(next_body, geometry, chunks[1]),
        in_specs=[smem, vmem, vmem, vmem, pl.BlockSpec(memory_space=pl.ANY)],
        out_specs=[vmem] * 2,
        out_shape=[parts[1], products[1]],
        compiler_params=params,
        name="next_chunk",
    )(l_atom, table, left, right, z_keep)
    send, product, z_other = lax.optimization_barrier((send, product, z_other))
    other = lax.ppermute(send, "core", swap)
    keep = own_part(1, product)
    count = chunks[1][1]
    rows = (count + 1) * owned
    joined = pl.pallas_call(
        functools.partial(join_body, owned, places, count),
        in_specs=[vmem] * 4,
        out_specs=vmem,
        out_shape=pltpu.VMEM((places * rows, LANES), F32),
        scratch_shapes=[pltpu.VMEM((places * n * owned, LANES), F32) for n in (1, count)],
        compiler_params=params,
        name="join_rows",
    )(z_keep, z_other, keep, other)
    tile = joined.reshape(places, rows, 1, LANES)
    got = lax.all_to_all(tile, ("zl", "x", "zh", "y"), split_axis=0, concat_axis=0, tiled=True)
    total = pl.pallas_call(
        functools.partial(sum_body, owned, groups, total_j, chunks),
        in_specs=[vmem],
        out_specs=vmem,
        out_shape=jax.ShapeDtypeStruct((owned, total_j, columns), F32),
        compiler_params=params,
        name="sum_sources",
    )(got.reshape(-1, LANES))
    return total[:, None]


def solution(mesh):
    fine = Mesh(mesh.devices.reshape(2, 4, 2, 2, 4), ("zl", "x", "core", "zh", "y"))
    ang, slab = ("zl", "x", "core"), ("zh", "y")
    in_specs = (P(ang, None, slab, None), P(), P(), P(), P(), P())
    out_specs = P(ang, slab, None, None)
    return jax.shard_map(local, mesh=fine, in_specs=in_specs, out_specs=out_specs, check_vma=False)
```
